256 devices in a mesh: enc: 8 (over z), kr: 8 (over x_lo, y), kc: 4 (over x_hi, core).
Axes of the slice: x: 4 (x_hi: 2, x_lo: 2; x = x_hi * 2 + x_lo), y: 4, z: 8, core: 2. Of those that a mesh axis runs over, the one named last changes fastest.
Arguments:
- inputs: bfloat16 [49152, 1024], P(('enc', 'kr', 'kc')), may hold values from -24 to 24
- w_first: bfloat16 [1024, 1024], replicated, may hold values from -0.1875 to 0.1875
- w_second: bfloat16 [1024, 64], replicated, may hold values from -0.1875 to 0.1875
- inv_length: float32 [64], replicated, may hold values from 0.05 to 1.8
- probes: bfloat16 [49152, 128], P(('enc', 'kr', 'kc')), may hold values from -6 to 6
- solves: bfloat16 [49152, 128], P(('enc', 'kr', 'kc')), may hold values from -6 to 6
Outputs:
- products: bfloat16 [49152, 128], P(('enc', 'kr', 'kc'))
- grad_first: float32 [1024, 1024], P(('enc', 'kr', 'kc'))
- grad_second: float32 [1024, 64], P(('enc', 'kr', 'kc'))
The draws below stay inside these ranges and needn't reach their ends.
All inputs are finite; a program needn't handle non-finite values.
Results may differ from the reference program's by a relative error of at most 0.007.
The reference program's roundings to bfloat16 on the way count: a program that leaves them out, or rounds other values in their place, can miss the bound.
Values may be sent and summed in bfloat16 or wider, within the bound.
A program may use at most 64 MiB of HBM per device.

```python
import math
import jax
import jax.numpy as jnp
from jax import lax

IN = 1024
HID = 1024
FEAT = 64
PROBES = 128
ROWS = 49152


def draw_inv_length(key, part):
    base_key = jax.random.fold_in(key, 7)
    pick_key, narrow_key, broad_key = jax.random.split(base_key, 3)
    ranking = jax.random.permutation(pick_key, FEAT)
    narrow_mask = ranking < FEAT // 4
    narrow_scale = jnp.exp(jax.random.uniform(narrow_key, (FEAT,), jnp.float32, math.log(0.9), math.log(1.8)))
    broad_scale = jnp.exp(jax.random.uniform(broad_key, (FEAT,), jnp.float32, math.log(0.05), math.log(0.3)))
    return jnp.where(narrow_mask, narrow_scale, broad_scale).astype(jnp.float32)


def strengthened(array, key, source, target, parts, factor):
    owner, partner = [(jnp.arange(array.shape[dim]) // (array.shape[dim] // parts)).reshape([-1 if axis == dim else 1 for axis in range(array.ndim)]) for dim in (source, target)]
    chosen = jax.random.permutation(key, parts)[partner]
    strong = (owner == chosen) | (owner == (partner + parts // 2) % parts)
    return jnp.where(strong, factor * array, array)


def level_of(stream_key, dims, cuts, low, top_value):
    def one(axis_at, parts):
        draws = jax.random.uniform(jax.random.fold_in(jax.random.fold_in(stream_key, 6), axis_at), (parts,), jnp.float32, low / len(cuts), top_value / len(cuts))
        return jnp.repeat(jnp.exp(draws), dims[axis_at] // parts).reshape((-1,) + (1,) * (len(dims) - axis_at - 1))

    loudness = one(*cuts[0])
    for cut in cuts[1:]:
        loudness = loudness * one(*cut)
    return loudness


def normal_values(rng, shape, scale, most, pieces=(), kind=jnp.bfloat16):
    drawn = jax.random.normal(rng, shape, jnp.float32) * scale
    if len(pieces) > 0:
        drawn = level_of(rng, shape, pieces, -0.22, 0.18) * drawn
    return jnp.clip(drawn, min=-most, max=most).astype(kind)


def bell_draw_with(own_key, dims, deviation, most, pieces, heavy, kind=jnp.bfloat16):
    drawn = deviation * jax.random.normal(own_key, dims, jnp.float32)
    if pieces:
        drawn = drawn * level_of(own_key, dims, pieces, -0.22, 0.18)
    return jnp.clip(strengthened(drawn, jax.random.fold_in(own_key, 3), *heavy), -most, most).astype(kind)


def setup_inputs(seed: int = 0) -> dict:
    key_list = jax.random.split(jax.random.key(seed), 7)
    inputs = bell_draw_with(key_list[0], (ROWS, IN), 1.0, 24.0, ((0, 256),), (0, 1, 256, 6.0))
    w_first = normal_values(key_list[1], (IN, HID), IN ** -0.5, 0.1875)
    w_second = normal_values(key_list[2], (HID, FEAT), HID ** -0.5, 0.1875)
    inv_length = draw_inv_length(jax.random.fold_in(key_list[6], 71), 0)
    probes = normal_values(key_list[4], (ROWS, PROBES), 1.0, 6.0, ((0, 256),))
    solves = normal_values(key_list[5], (ROWS, PROBES), 1.0, 6.0, ((0, 256),))
    return {"inputs": inputs, "w_first": w_first, "w_second": w_second, "inv_length": inv_length, "probes": probes, "solves": solves}


probe_gain = 0.5
loss_gain = 0.02

def contract_inner(left, right):
    return lax.dot_general(left, right, (((1,), (1,)), ((), ())), preferred_element_type=jnp.float32)

def contract_outer(left, right):
    return lax.dot_general(left, right, (((0,), (0,)), ((), ())), preferred_element_type=jnp.float32)

def reference(inputs, w_first, w_second, inv_length, probes, solves):
    pre = jnp.dot(inputs, w_first, preferred_element_type=jnp.float32)
    hidden = jax.nn.silu(pre).astype(jnp.bfloat16)
    features = jnp.dot(hidden, w_second, preferred_element_type=jnp.float32)
    scaled = (features * inv_length[None, :]).astype(jnp.bfloat16)
    widened = scaled.astype(jnp.float32)
    norms = lax.optimization_barrier(jnp.sum(widened * widened, axis=1))
    total = scaled.shape[0]
    block_rows = min(512, total)
    count = total // block_rows

    def per_block(index):
        offset = (index * block_rows).astype(jnp.int32)
        row_feat = lax.dynamic_slice_in_dim(scaled, offset, block_rows, 0)
        row_norm = lax.dynamic_slice_in_dim(norms, offset, block_rows, 0)
        row_probe = lax.dynamic_slice_in_dim(probes, offset, block_rows, 0)
        row_solve = lax.dynamic_slice_in_dim(solves, offset, block_rows, 0)
        cross = contract_inner(row_feat, scaled)
        kernel = jnp.exp(-0.5 * (row_norm[:, None] + norms[None, :] - 2.0 * cross))
        vsum = jnp.dot(kernel.astype(jnp.bfloat16), probes, preferred_element_type=jnp.float32)
        first = kernel * contract_inner(row_solve, probes)
        second = kernel * contract_inner(row_probe, solves)
        sums = lax.optimization_barrier(jnp.sum(first, axis=1)) + lax.optimization_barrier(jnp.sum(second, axis=1))
        mixed = jnp.dot(first.astype(jnp.bfloat16), scaled, preferred_element_type=jnp.float32) + jnp.dot(second.astype(jnp.bfloat16), scaled, preferred_element_type=jnp.float32)
        return (vsum, mixed, sums)
    vsum, mixed, sums = lax.map(per_block, jnp.arange(count, dtype=jnp.int32))
    vsum = vsum.reshape(total, probes.shape[1])
    mixed = mixed.reshape(total, scaled.shape[1])
    sums = sums.reshape(total)
    products = (vsum * probe_gain).astype(jnp.bfloat16)
    lscale = loss_gain / math.sqrt(probes.shape[1])
    dfeat = -lscale * inv_length[None, :] * (sums[:, None] * widened - mixed)
    dfeat_half = dfeat.astype(jnp.bfloat16)
    grad_second = contract_outer(hidden, dfeat_half)
    back_hidden = contract_inner(dfeat_half, w_second)
    sigma = jax.nn.sigmoid(pre)
    dpre = (back_hidden * sigma * (1.0 + pre * (1.0 - sigma))).astype(jnp.bfloat16)
    grad_first = contract_outer(inputs, dpre)
    return (products, grad_first, grad_second)
```

```python
import functools
import math

import jax
import jax.numpy as jnp
from jax import lax
from jax.experimental import pallas as pl
from jax.experimental.pallas import tpu as pltpu
from jax.sharding import PartitionSpec as P

probe_gain = 0.5
loss_gain = 0.02

ROWS = 192
HALF = ROWS // 2
IN = 1024
HID = 1024
FEAT = 64
PROBES = 128
PLANE = 16
COLS = 16
WIDTH = COLS * ROWS
GROUP = 4
SLICE = HID // GROUP
GROWS = GROUP * ROWS
LANES = SLICE // 128
TILES = 8 * LANES + 4
LOG2E = 1.4426950408889634
MESH = pl.DeviceIdType.MESH
f32 = jnp.float32
bf16 = jnp.bfloat16


def dot(left, right):
    return jnp.dot(left, right, preferred_element_type=f32)


def dot_nt(left, right):
    return lax.dot_general(left, right, (((1,), (1,)), ((), ())), preferred_element_type=f32)


def split3(value):
    one = value.astype(bf16)
    rest = value - one.astype(f32)
    two = rest.astype(bf16)
    three = (rest - two.astype(f32)).astype(bf16)
    return one, two, three


def unpack_rows(packed):
    return jnp.concatenate([packed[:, :FEAT], packed[:, FEAT:]], axis=0)


def pack_rows(value):
    half = value.shape[0] // 2
    return jnp.concatenate([value[:half], value[half:]], axis=1)


def half_norms(wide):
    return (-0.5 * LOG2E) * jnp.sum(wide * wide, axis=1, keepdims=True)


def extras(norms, own, other):
    one, two, three = split3(norms)
    lane = lax.broadcasted_iota(jnp.int32, (norms.shape[0], FEAT), 1)
    filled = jnp.where((lane >= other) & (lane < other + 3), 1.0, 0.0)
    filled = jnp.where(lane == own, one.astype(f32), filled)
    filled = jnp.where(lane == own + 1, two.astype(f32), filled)
    filled = jnp.where(lane == own + 2, three.astype(f32), filled)
    return filled.astype(bf16)


def kernel(
    inputs, w_first, w_second, inv_length, probes, solves,
    products, grad_first, grad_second,
    row_p, row_s, row_u, col_p, col_s, col_u, cross_t, inner_t, mix,
    out_v, out_d, got_v, got_d,
    group_x, group_xt, factor, hidden_t, group_d,
    chunks, got_chunks, pieces, got_pieces,
    row_send, row_recv, col_send, col_recv, side_send, side_recv,
    out_send, out_recv, x_send, x_recv, d_send, d_recv,
    chunk_send, chunk_recv, piece_send, piece_recv,
):
    z = lax.axis_index("enc")
    kr = lax.axis_index("kr")
    kc = lax.axis_index("kc")
    y = lax.rem(kr, 4)
    x = 2 * lax.div(kc, 2) + lax.div(kr, 4)
    core = lax.rem(kc, 2)

    def device(x, y, z, core):
        return (z, 4 * lax.rem(x, 2) + y, 2 * lax.div(x, 2) + core)

    def plane_peer(step, sign):
        dx = lax.div(step, 4)
        dy = lax.rem(step, 4)
        px = lax.rem(x + 4 + sign * dx, 4)
        py = lax.rem(y + 4 + sign * dy, 4)
        return px, py

    def column_peer(step):
        return lax.rem(z + lax.div(step, 2), 8), lax.rem(core + lax.rem(step, 2), 2)

    def remote(src, dst, send, recv, target):
        return pltpu.make_async_remote_copy(
            src_ref=src, dst_ref=dst, send_sem=send, recv_sem=recv,
            device_id=target, device_id_type=MESH,
        )

    me = (z, kr, kc)
    sibling = device(x, y, z, 1 - core)
    up = device(x, y, lax.rem(z + 1, 8), core)
    down = device(x, y, lax.rem(z + 7, 8), core)
    z_low = lax.rem(z, 2)
    member = 2 * z_low + core

    barrier = pltpu.get_barrier_semaphore()

    def greet_plane(step, carry):
        px, py = plane_peer(step, 1)
        pl.semaphore_signal(barrier, inc=1, device_id=device(px, py, z, core), device_id_type=MESH)
        return carry

    def greet_column(step, carry):
        pz, pc = column_peer(step)
        pl.semaphore_signal(barrier, inc=1, device_id=device(x, y, pz, pc), device_id_type=MESH)
        return carry

    lax.fori_loop(1, PLANE, greet_plane, 0)
    lax.fori_loop(1, COLS, greet_column, 0)
    pl.semaphore_wait(barrier, 30)

    def ring(which, source, slot, part_up):
        buffers = (col_p, col_s, col_u)
        buffer = buffers[which]
        if part_up and slot < 4:
            yield remote(source, buffer.at[slot + 1], col_send.at[which, slot], col_recv.at[which, slot + 1], up)
        if slot == 0 or 5 <= slot < 7:
            later = 5 if slot == 0 else slot + 1
            yield remote(source, buffer.at[later], col_send.at[which, slot + 4 if slot == 0 else slot], col_recv.at[which, later], down)
        yield remote(source, buffer.at[8 + slot], side_send.at[which, slot], side_recv.at[which, slot], sibling)

    sources = (probes, solves)
    for which in range(2):
        for copy in ring(which, sources[which], 0, True):
            copy.start()

    def row_copy(which, step):
        px, py = plane_peer(step, -1)
        source = (probes, solves, col_u.at[0])[which]
        return remote(
            source, (row_p, row_s, row_u)[which].at[step],
            row_send.at[which, step], row_recv.at[which, step], device(px, py, z, core),
        )

    def send_rows(step, carry):
        row_copy(0, step).start()
        row_copy(1, step).start()
        return carry

    lax.fori_loop(1, PLANE, send_rows, 0)

    def encode(block, total):
        start = pl.multiple_of(block * 256, 256)
        pre = dot(inputs[...], w_first[:, pl.ds(start, 256)])
        hidden = (pre * jax.nn.sigmoid(pre)).astype(bf16)
        hidden_t[pl.ds(start, 256), :] = hidden.T
        return total + dot(hidden, w_second[pl.ds(start, 256), :])

    features = lax.fori_loop(0, HID // 256, encode, jnp.zeros((ROWS, FEAT), f32))
    scaled = (features * inv_length[...]).astype(bf16)
    packed = pack_rows(scaled)
    col_u[0] = packed
    row_u[0] = packed
    for copy in ring(2, col_u.at[0], 0, True):
        copy.start()

    def send_features(step, carry):
        row_copy(2, step).start()
        return carry

    lax.fori_loop(1, PLANE, send_features, 0)

    def group_copy(step, source, buffer, send, recv):
        other = lax.rem(member + step, GROUP)
        pz = z - z_low + lax.div(other, 2)
        return remote(source, buffer.at[member], send.at[step], recv.at[step], device(x, y, pz, lax.rem(other, 2)))

    def group_wait(step, source, buffer, send, recv):
        other = lax.rem(member + GROUP - step, GROUP)
        remote(source, buffer.at[other], send.at[step], recv.at[step], me).wait_recv()

    col_p[0] = probes[...]
    col_s[0] = solves[...]
    row_p[0] = probes[...]
    row_s[0] = solves[...]
    group_x[member] = inputs[...]

    for slot in (1, 5, 2, 6, 3, 7, 4):
        for which in range(3):
            buffer = (col_p, col_s, col_u)[which]
            remote(buffer.at[slot], buffer.at[slot], col_send.at[which, 0], col_recv.at[which, slot], me).wait_recv()
            for copy in ring(which, buffer.at[slot], slot, slot < 5):
                copy.start()
    for step in range(1, GROUP):
        group_copy(step, inputs, group_x, x_send, x_recv).start()
    for slot in range(8):
        for which in range(3):
            buffer = (col_p, col_s, col_u)[which]
            remote(buffer.at[slot], buffer.at[8 + slot], side_send.at[which, slot], side_recv.at[which, slot], me).wait_recv()

    def prepare(pair, carry):
        slot = 2 * pair
        start = pl.multiple_of(slot * ROWS, 2 * ROWS)
        u = jnp.concatenate([unpack_rows(col_u[slot]), unpack_rows(col_u[slot + 1])], axis=0)
        wide = u.astype(f32)
        one, two, three = split3(wide * LOG2E)
        tail = extras(half_norms(wide), 3, 0)
        operand = jnp.concatenate([one, two, three, tail], axis=1)
        cross_t[:, pl.ds(start, 2 * ROWS)] = operand.T
        p = jnp.concatenate([col_p[slot], col_p[slot + 1]], axis=0)
        s = jnp.concatenate([col_s[slot], col_s[slot + 1]], axis=0)
        inner_t[pl.ds(0, PROBES), pl.ds(start, 2 * ROWS)] = p.T
        inner_t[pl.ds(PROBES, PROBES), pl.ds(start, 2 * ROWS)] = s.T
        mix[pl.ds(start, 2 * ROWS), :] = u
        return carry

    lax.fori_loop(0, COLS // 2, prepare, 0)

    def out_copy(step, which):
        px, py = plane_peer(step, 1)
        source = (out_v, out_d)[which]
        target = (got_v, got_d)[which]
        return remote(
            source.at[step], target.at[step], out_send.at[which, step], out_recv.at[which, step],
            device(px, py, z, core),
        )

    def row_block(step, carry):
        @pl.when(step > 0)
        def _():
            for which in range(3):
                row_copy(which, step).wait_recv()

        u = unpack_rows(row_u[step])
        wide = u.astype(f32)
        left = jnp.concatenate([u, u, u, extras(half_norms(wide), 0, 3)], axis=1)
        inner = jnp.concatenate([row_s[step], row_p[step]], axis=1)
        vsum = jnp.zeros((ROWS, PROBES), f32)
        mixed = jnp.zeros((ROWS, FEAT), f32)
        sums = jnp.zeros((ROWS, 2 * FEAT), f32)
        block = 1024
        for start in range(0, WIDTH, block):
            value = jnp.exp2(dot(left, cross_t[:, start:start + block]))
            both = value * dot(inner, inner_t[:, start:start + block])
            for lane in range(0, block, 2 * FEAT):
                sums = sums + both[:, lane:lane + 2 * FEAT]
            both = both.astype(bf16)
            p = col_p[...].reshape(WIDTH, PROBES)[start:start + block]
            vsum = vsum + dot(value.astype(bf16), p)
            mixed = mixed + dot(both, mix[start:start + block, :])
        part = jnp.sum(sums, axis=1, keepdims=True) * wide - mixed
        out_v[step] = vsum.astype(bf16)
        out_d[step] = pack_rows(part).astype(bf16)

        @pl.when(step > 0)
        def _():
            out_copy(step, 0).start()
            out_copy(step, 1).start()

        return carry

    lax.fori_loop(0, PLANE, row_block, 0)

    for step in range(1, GROUP):
        group_wait(step, inputs, group_x, x_send, x_recv)
    here = pl.multiple_of(member * SLICE, SLICE)

    def group_rows(pair, carry):
        rows = group_x[pl.ds(2 * pair, 2)].reshape(2 * ROWS, IN)
        start = pl.multiple_of(pair * 2 * ROWS, 2 * ROWS)
        group_xt[:, pl.ds(start, 2 * ROWS)] = rows.T
        pre = dot(rows, w_first[:, pl.ds(here, SLICE)])
        sigma = jax.nn.sigmoid(pre)
        factor[pl.ds(start, 2 * ROWS), :] = sigma * (1.0 + pre * (1.0 - sigma))
        return carry

    lax.fori_loop(0, GROUP // 2, group_rows, 0)

    def add_up(step, totals):
        for which in range(2):
            out_copy(step, which).wait_recv()
        return totals[0] + got_v[step].astype(f32), totals[1] + got_d[step].astype(f32)

    vsum, part = lax.fori_loop(1, PLANE, add_up, (out_v[0].astype(f32), out_d[0].astype(f32)))
    products[...] = (vsum * probe_gain).astype(bf16)
    lscale = loss_gain / math.sqrt(PROBES)
    length = inv_length[...]
    dfeat = part * (-lscale * jnp.concatenate([length, length], axis=1))
    packed_d = dfeat.astype(bf16)
    group_d[member] = packed_d
    for step in range(1, GROUP):
        group_copy(step, group_d.at[member], group_d, d_send, d_recv).start()

    second = dot(hidden_t[...], unpack_rows(packed_d))
    low = jnp.concatenate([second[: HID // 2], second[HID // 2:]], axis=1).astype(bf16)
    for far in range(4):
        tile = 8 * LANES + far
        chunks[:, tile * 8:tile * 8 + 8, :] = low[128 * far:128 * far + 128].reshape(PLANE, 8, 128)

    for step in range(1, GROUP):
        group_wait(step, group_d.at[member], group_d, d_send, d_recv)
    whole_d = jnp.concatenate([unpack_rows(group_d[item]) for item in range(GROUP)], axis=0)
    back = dot_nt(whole_d, w_second[pl.ds(here, SLICE), :])
    dpre = (back * factor[...]).astype(bf16)
    for far in range(8):
        first = dot(group_xt[128 * far:128 * far + 128, :], dpre).astype(bf16)
        for lane in range(LANES):
            tile = far * LANES + lane
            chunks[:, tile * 8:tile * 8 + 8, :] = first[:, 128 * lane:128 * lane + 128].reshape(PLANE, 8, 128)

    def place(px, py):
        return 2 * (4 * lax.rem(px, 2) + py) + lax.div(px, 2)

    def chunk_copy(step):
        px, py = plane_peer(step, 1)
        return remote(
            chunks.at[place(px, py)], got_chunks.at[step], chunk_send.at[step], chunk_recv.at[step],
            device(px, py, z, core),
        )

    def send_chunk(step, carry):
        chunk_copy(step).start()
        return carry

    lax.fori_loop(1, PLANE, send_chunk, 0)

    def add_chunk(step, total):
        chunk_copy(step).wait_recv()
        return total + got_chunks[step].astype(f32)

    summed = lax.fori_loop(1, PLANE, add_chunk, chunks[place(x, y)].astype(f32))

    depth = 8 * LANES
    for far in range(8):
        extra = 8 * depth + 8 * (far % 4)
        pieces[far] = jnp.concatenate(
            [summed[depth * far:depth * far + depth], summed[extra:extra + 8]], axis=0
        )

    own_slot = 2 * z + core

    def piece_copy(step):
        pz, pc = column_peer(step)
        return remote(
            pieces.at[pz], got_pieces.at[own_slot], piece_send.at[step], piece_recv.at[step],
            device(x, y, pz, pc),
        )

    def send_piece(step, carry):
        piece_copy(step).start()
        return carry

    lax.fori_loop(1, COLS, send_piece, 0)
    got_pieces[own_slot] = pieces[z]

    def wait_piece(step, carry):
        pz = lax.rem(z + 8 - lax.div(step, 2), 8)
        pc = lax.rem(core + lax.rem(step, 2), 2)
        remote(pieces.at[z], got_pieces.at[2 * pz + pc], piece_send.at[step], piece_recv.at[step], me).wait_recv()
        return carry

    lax.fori_loop(1, COLS, wait_piece, 0)
    strips = []
    tail = jnp.zeros((8, 128), f32)
    for item in range(GROUP):
        total = got_pieces[item]
        for other in range(item + GROUP, COLS, GROUP):
            total = total + got_pieces[other]
        strips += [total[8 * lane:8 * lane + 8] for lane in range(LANES)]
        tail = tail + total[depth:depth + 8]
    full = jnp.concatenate(strips, axis=1)
    grad_first[...] = jnp.where(core == 0, full[:4], full[4:])
    tail = jnp.where(z < 4, tail[:, :FEAT], tail[:, FEAT:])
    grad_second[...] = jnp.where(core == 0, tail[:4], tail[4:])

    for which in range(3):
        source = (probes, solves, col_u.at[0])[which]
        for copy in ring(which, source, 0, True):
            copy.wait_send()
        for slot in range(1, 8):
            for copy in ring(which, (col_p, col_s, col_u)[which].at[slot], slot, slot < 5):
                copy.wait_send()

    def finish_plane(step, carry):
        for which in range(3):
            row_copy(which, step).wait_send()
        for which in range(2):
            out_copy(step, which).wait_send()
        chunk_copy(step).wait_send()
        return carry

    lax.fori_loop(1, PLANE, finish_plane, 0)
    for step in range(1, GROUP):
        group_copy(step, inputs, group_x, x_send, x_recv).wait_send()
        group_copy(step, group_d.at[member], group_d, d_send, d_recv).wait_send()

    def finish_column(step, carry):
        piece_copy(step).wait_send()
        return carry

    lax.fori_loop(1, COLS, finish_column, 0)


def local(inputs, w_first, w_second, inv_length, probes, solves):
    vmem = pl.BlockSpec(memory_space=pltpu.VMEM)
    dma = pltpu.SemaphoreType.DMA
    return pl.pallas_call(
        kernel,
        out_shape=(
            jax.ShapeDtypeStruct((ROWS, PROBES), bf16),
            jax.ShapeDtypeStruct((4, HID), f32),
            jax.ShapeDtypeStruct((4, FEAT), f32),
        ),
        in_specs=[vmem] * 6,
        out_specs=(vmem, vmem, vmem),
        scratch_shapes=[
            pltpu.VMEM((PLANE, ROWS, PROBES), bf16),
            pltpu.VMEM((PLANE, ROWS, PROBES), bf16),
            pltpu.VMEM((PLANE, HALF, 2 * FEAT), bf16),
            pltpu.VMEM((COLS, ROWS, PROBES), bf16),
            pltpu.VMEM((COLS, ROWS, PROBES), bf16),
            pltpu.VMEM((COLS, HALF, 2 * FEAT), bf16),
            pltpu.VMEM((4 * FEAT, WIDTH), bf16),
            pltpu.VMEM((2 * PROBES, WIDTH), bf16),
            pltpu.VMEM((WIDTH, FEAT), bf16),
            pltpu.VMEM((PLANE, ROWS, PROBES), bf16),
            pltpu.VMEM((PLANE, HALF, 2 * FEAT), bf16),
            pltpu.VMEM((PLANE, ROWS, PROBES), bf16),
            pltpu.VMEM((PLANE, HALF, 2 * FEAT), bf16),
            pltpu.VMEM((GROUP, ROWS, IN), bf16),
            pltpu.VMEM((IN, GROWS), bf16),
            pltpu.VMEM((GROWS, SLICE), f32),
            pltpu.VMEM((HID, ROWS), bf16),
            pltpu.VMEM((GROUP, HALF, 2 * FEAT), bf16),
            pltpu.VMEM((PLANE, TILES * 8, 128), bf16),
            pltpu.VMEM((PLANE, TILES * 8, 128), bf16),
            pltpu.VMEM((8, 8 * LANES + 8, 128), f32),
            pltpu.VMEM((COLS, 8 * LANES + 8, 128), f32),
            dma((3, PLANE)), dma((3, PLANE)),
            dma((3, 8)), dma((3, 8)), dma((3, 8)), dma((3, 8)),
            dma((2, PLANE)), dma((2, PLANE)),
            dma((GROUP,)), dma((GROUP,)), dma((GROUP,)), dma((GROUP,)),
            dma((PLANE,)), dma((PLANE,)), dma((COLS,)), dma((COLS,)),
        ],
        compiler_params=pltpu.CompilerParams(
            collective_id=0, has_side_effects=True, vmem_limit_bytes=56 * 1024 * 1024
        ),
        name="gradient_step",
    )(inputs, w_first, w_second, inv_length.reshape(1, FEAT), probes, solves)


def solution(mesh):
    rows = P(("enc", "kr", "kc"), None)
    return jax.shard_map(
        local, mesh=mesh, in_specs=(rows, P(), P(), P(), rows, rows),
        out_specs=(rows, rows, rows), check_vma=False,
    )
```

```python
import functools
import math

import jax
import jax.numpy as jnp
from jax import lax
from jax.experimental import pallas as pl
from jax.experimental.pallas import tpu as pltpu
from jax.sharding import PartitionSpec as P

probe_gain = 0.5
loss_gain = 0.02

ROWS = 192
HALF = ROWS // 2
IN = 1024
HID = 1024
FEAT = 64
PROBES = 128
PLANE = 16
COLS = 16
WIDTH = COLS * ROWS
GROUP = 4
SLICE = HID // GROUP
GROWS = GROUP * ROWS
LANES = SLICE // 128
TILES = 8 * LANES + 4
LOG2E = 1.4426950408889634
MESH = pl.DeviceIdType.MESH
f32 = jnp.float32
bf16 = jnp.bfloat16


def dot(left, right):
    return jnp.dot(left, right, preferred_element_type=f32)


NEAR = 5
EARLY = 5
STEPS = (
    (0, 0), (0, 1), (0, 3), (1, 0), (3, 0), (1, 1), (3, 3), (1, 3),
    (3, 1), (0, 2), (2, 0), (2, 1), (2, 3), (1, 2), (3, 2), (2, 2),
)
PAIR = 2 * ROWS
CHUNK = 4 * ROWS
OWN = 12


def dot_nt(left, right):
    return lax.dot_general(left, right, (((1,), (1,)), ((), ())), preferred_element_type=f32)


def split3(value):
    one = value.astype(bf16)
    rest = value - one.astype(f32)
    two = rest.astype(bf16)
    three = (rest - two.astype(f32)).astype(bf16)
    return one, two, three


def unpack_rows(packed):
    return jnp.concatenate([packed[:, :FEAT], packed[:, FEAT:]], axis=0)


def pack_rows(value):
    half = value.shape[0] // 2
    return jnp.concatenate([value[:half], value[half:]], axis=1)


def half_norms(wide):
    return (-0.5 * LOG2E) * jnp.sum(wide * wide, axis=1, keepdims=True)


def extras(norms, own, other):
    one, two, three = split3(norms)
    lane = lax.broadcasted_iota(jnp.int32, (norms.shape[0], FEAT), 1)
    filled = jnp.where((lane >= other) & (lane < other + 3), 1.0, 0.0)
    filled = jnp.where(lane == own, one.astype(f32), filled)
    filled = jnp.where(lane == own + 1, two.astype(f32), filled)
    filled = jnp.where(lane == own + 2, three.astype(f32), filled)
    return filled.astype(bf16)


def kernel(
    inputs_hbm, w_first_hbm, w_second_hbm, inv_length, probes_hbm, solves_hbm,
    products, grad_first, grad_second,
    w_first, w_second, row_p, row_s, row_u, col_p, col_s, col_u, cross_t, inner_t, mix,
    left_near, near_v, near_m, near_s, out_v, out_d, got_v, got_d,
    group_x, group_xt, factor, hidden_t, group_d,
    chunks, got_chunks, pieces, got_pieces,
    load_sem, row_send, row_recv, up_send, down_send, side_send, col_recv,
    out_send, out_recv, x_send, x_recv, d_send, d_recv,
    chunk_send, chunk_recv, piece_send, piece_recv,
):
    z = lax.axis_index("enc")
    kr = lax.axis_index("kr")
    kc = lax.axis_index("kc")
    y = lax.rem(kr, 4)
    x = 2 * lax.div(kc, 2) + lax.div(kr, 4)
    core = lax.rem(kc, 2)

    def device(x, y, z, core):
        return (z, 4 * lax.rem(x, 2) + y, 2 * lax.div(x, 2) + core)

    def moved(dx, dy, sign):
        return lax.rem(x + 4 + sign * dx, 4), lax.rem(y + 4 + sign * dy, 4)

    def plane_peer(step, sign):
        return moved(lax.div(step, 4), lax.rem(step, 4), sign)

    def column_peer(step):
        return lax.rem(z + lax.div(step, 2), 8), lax.rem(core + lax.rem(step, 2), 2)

    def remote(src, dst, send, recv, target):
        return pltpu.make_async_remote_copy(
            src_ref=src, dst_ref=dst, send_sem=send, recv_sem=recv,
            device_id=target, device_id_type=MESH,
        )

    me = (z, kr, kc)
    sibling = device(x, y, z, 1 - core)
    up = device(x, y, lax.rem(z + 1, 8), core)
    down = device(x, y, lax.rem(z + 7, 8), core)
    z_low = lax.rem(z, 2)
    member = 2 * z_low + core

    barrier = pltpu.get_barrier_semaphore()

    def greet_plane(step, carry):
        px, py = plane_peer(step, 1)
        pl.semaphore_signal(barrier, inc=1, device_id=device(px, py, z, core), device_id_type=MESH)
        return carry

    def greet_column(step, carry):
        pz, pc = column_peer(step)
        pl.semaphore_signal(barrier, inc=1, device_id=device(x, y, pz, pc), device_id_type=MESH)
        return carry

    lax.fori_loop(1, PLANE, greet_plane, 0)
    lax.fori_loop(1, COLS, greet_column, 0)

    loads = [
        pltpu.make_async_copy(source, target, load_sem.at[index])
        for index, (source, target) in enumerate((
            (inputs_hbm, group_x.at[member]), (w_first_hbm, w_first), (w_second_hbm, w_second),
            (probes_hbm, col_p.at[OWN]), (solves_hbm, col_s.at[OWN]),
            (probes_hbm, row_p.at[0]), (solves_hbm, row_s.at[0]),
        ))
    ]
    for load in loads:
        load.start()
    for load in loads:
        load.wait()

    def encode(block, total):
        start = pl.multiple_of(block * 256, 256)
        pre = dot(group_x[member], w_first[:, pl.ds(start, 256)])
        hidden = (pre * jax.nn.sigmoid(pre)).astype(bf16)
        hidden_t[pl.ds(start, 256), :] = hidden.T
        return total + dot_nt(hidden, w_second[:, pl.ds(start, 256)])

    features = lax.fori_loop(0, HID // 256, encode, jnp.zeros((ROWS, FEAT), f32))
    scaled = (features * inv_length[...]).astype(bf16)
    packed = pack_rows(scaled)
    col_u[OWN] = packed
    row_u[0] = packed

    pl.semaphore_wait(barrier, 30)

    columns = (col_u, col_p, col_s)
    rows = (row_u, row_p, row_s)

    def up_slot(far):
        if isinstance(far, int):
            return (OWN, 0, 4, 8, OWN + 2)[far]
        return jnp.where(far == 4, OWN + 2, 4 * far - 4)

    def down_slot(far):
        if isinstance(far, int):
            return (OWN, 1, 5, 9)[far]
        return 4 * far - 3

    def up_copy(which, far):
        buffer = columns[which]
        return remote(
            buffer.at[up_slot(far)], buffer.at[up_slot(far + 1)],
            up_send.at[which, far], col_recv.at[which, up_slot(far + 1)], up,
        )

    def down_copy(which, far):
        buffer = columns[which]
        return remote(
            buffer.at[down_slot(far)], buffer.at[down_slot(far + 1)],
            down_send.at[which, far], col_recv.at[which, down_slot(far + 1)], down,
        )

    def side_copy(which, slot, there):
        buffer = columns[which]
        return remote(
            buffer.at[slot], buffer.at[there], side_send.at[which, slot], col_recv.at[which, there], sibling,
        )

    def column_wait(which, slot):
        buffer = columns[which]
        remote(buffer.at[slot], buffer.at[slot], side_send.at[which, 0], col_recv.at[which, slot], me).wait_recv()

    def row_send_on(which, source, dx, dy, here):
        slot = STEPS.index(here)
        px, py = moved(dx, dy, 1)
        return remote(
            rows[which].at[STEPS.index(source)], rows[which].at[slot],
            row_send.at[which, slot], row_recv.at[which, slot], device(px, py, z, core),
        )

    def row_wait(which, step):
        remote(
            rows[which].at[0], rows[which].at[step],
            row_send.at[which, step], row_recv.at[which, step], me,
        ).wait_recv()

    ways = ((1, 3), (1, 1), (0, 3))

    def offset(axis, along, across):
        return (along, across) if axis == 0 else (across, along)

    def spread(which, block):
        first, turn = ways[which]
        second = 1 - first
        along, across = block[first], block[second]
        moves = []
        if across == 0:
            if along == 0:
                moves += [(first, 1), (first, 3)]
            elif along == (4 - turn) % 4:
                moves.append((first, turn))
            moves += [(second, 1), (second, 3)]
        elif across == (4 - turn) % 4:
            moves.append((second, turn))
        for axis, way in moves:
            here = [block[0], block[1]]
            here[axis] = (here[axis] - way) % 4
            row_send_on(which, block, *offset(axis, way, 0), tuple(here)).start()

    waited = set()

    def take(which, block):
        waited.add((which, block))
        row_wait(which, STEPS.index(block))
        spread(which, block)

    def wave(level):
        for which in range(3):
            for block in STEPS[1:]:
                first, turn = ways[which]
                far = [0 if item == 0 else 2 if item == 2 else 1 for item in block]
                goes_on = block[1 - first] == 0 or block[1 - first] == (4 - turn) % 4
                if sum(far) == level and goes_on:
                    take(which, block)

    for which in range(3):
        up_copy(which, 0).start()
        down_copy(which, 0).start()
        spread(which, (0, 0))
        side_copy(which, OWN, OWN + 1).start()

    def advance(far):
        for which in range(3):
            here = up_slot(far)
            column_wait(which, here)

            @pl.when(far < 4)
            def _():
                up_copy(which, far).start()

            side_copy(which, here, jnp.where(far == 4, OWN + 3, 4 * far - 2)).start()

            @pl.when(far < 4)
            def _():
                column_wait(which, down_slot(far))

                @pl.when(far < 3)
                def _():
                    down_copy(which, far).start()

                side_copy(which, down_slot(far), 4 * far - 1).start()

    def group_copy(step, source, buffer, send, recv):
        other = lax.rem(member + step, GROUP)
        pz = z - z_low + lax.div(other, 2)
        return remote(source, buffer.at[member], send.at[step], recv.at[step], device(x, y, pz, lax.rem(other, 2)))

    def group_wait(step, source, buffer, send, recv):
        other = lax.rem(member + GROUP - step, GROUP)
        remote(source, buffer.at[other], send.at[step], recv.at[step], me).wait_recv()

    inputs = group_x.at[member]

    def row_operand(step):
        wide = unpack_rows(row_u[step]).astype(f32)
        u = wide.astype(bf16)
        return jnp.concatenate([u, u, u, extras(half_norms(wide), 0, 3)], axis=1), wide

    near_v[...] = jnp.zeros_like(near_v)
    near_m[...] = jnp.zeros_like(near_m)
    near_s[...] = jnp.zeros_like(near_s)
    wave(1)
    advance(1)
    for block in STEPS[1:NEAR]:
        for which in range(3):
            if (which, block) not in waited:
                take(which, block)

    def near_row(step, carry):
        left_near[pl.ds(pl.multiple_of(step * ROWS, ROWS), ROWS), :] = row_operand(step)[0]
        return carry

    lax.fori_loop(0, NEAR, near_row, 0)

    def prepare(pair):
        slot = 2 * pair
        start = pl.multiple_of(slot * ROWS, PAIR)
        u = jnp.concatenate([unpack_rows(col_u[slot]), unpack_rows(col_u[slot + 1])], axis=0)
        wide = u.astype(f32)
        one, two, three = split3(wide * LOG2E)
        tail = extras(half_norms(wide), 3, 0)
        operand = jnp.concatenate([one, two, three, tail], axis=1)
        cross_t[:, pl.ds(start, PAIR)] = operand.T
        p = jnp.concatenate([col_p[slot], col_p[slot + 1]], axis=0)
        s = jnp.concatenate([col_s[slot], col_s[slot + 1]], axis=0)
        inner_t[pl.ds(0, PROBES), pl.ds(start, PAIR)] = p.T
        inner_t[pl.ds(PROBES, PROBES), pl.ds(start, PAIR)] = s.T
        mix[pl.ds(start, PAIR), :] = u

    def tile(left, inner, start, size, p, u):
        value = jnp.exp2(dot(left, cross_t[:, pl.ds(start, size)]))
        both = value * dot(inner, inner_t[:, pl.ds(start, size)])
        sums = both[:, :128]
        for lane in range(128, size, 128):
            sums = sums + both[:, lane:lane + 128]
        return dot(value.astype(bf16), p), dot(both.astype(bf16), u), sums

    def near_tile(low, high, chunk):
        size = (high - low) * ROWS
        here = pl.ds(low * ROWS, size)
        start = pl.multiple_of(chunk * CHUNK, CHUNK)
        inner = jnp.concatenate(
            [row_s[low:high].reshape(size, PROBES), row_p[low:high].reshape(size, PROBES)], axis=1
        )
        p = col_p[pl.ds(4 * chunk, 4)].reshape(CHUNK, PROBES)
        vsum, mixed, sums = tile(left_near[here, :], inner, start, CHUNK, p, mix[pl.ds(start, CHUNK), :])
        near_v[here, :] += vsum
        near_m[here, :] += mixed
        near_s[here, :] += sums

    def table(step, values):
        if isinstance(step, int):
            return values[step]
        total = 0
        for index, value in enumerate(values):
            if value:
                total = total + jnp.where(step == index, value, 0)
        return total

    def out_copy(step, which):
        dx = table(step, [item[0] for item in STEPS])
        dy = table(step, [item[1] for item in STEPS])
        px, py = moved(dx, dy, 1)
        source = (out_v, out_d)[which]
        target = (got_v, got_d)[which]
        return remote(
            source.at[step], target.at[step], out_send.at[which, step], out_recv.at[which, step],
            device(px, py, z, core),
        )

    def finish_rows(step, vsum, mixed, sums, wide):
        part = jnp.sum(sums, axis=1, keepdims=True) * wide - mixed
        out_v[step] = vsum.astype(bf16)
        out_d[step] = pack_rows(part).astype(bf16)

        @pl.when(step > 0)
        def _():
            out_copy(step, 0).start()
            out_copy(step, 1).start()

    def near_out(step, carry):
        here = pl.ds(pl.multiple_of(step * ROWS, ROWS), ROWS)
        wide = unpack_rows(row_u[step]).astype(f32)
        finish_rows(step, near_v[here, :], near_m[here, :], near_s[here, :], wide)
        return carry

    def near_chunk(far, carry):
        @pl.when(far <= 4)
        def _():
            for which in range(3):
                @pl.when(far < 4)
                def _():
                    column_wait(which, 4 * far - 2)
                    column_wait(which, 4 * far - 1)

                @pl.when(far == 4)
                def _():
                    column_wait(which, OWN + 1)
                    column_wait(which, OWN + 3)

            prepare(2 * far - 2)
            prepare(2 * far - 1)
            near_tile(0, NEAR, far - 1)

        @pl.when(far == 4)
        def _():
            lax.fori_loop(0, NEAR, near_out, 0)

        @pl.when(far < 4)
        def _():
            advance(far + 1)

        @pl.when(far == 1)
        def _():
            wave(2)

        @pl.when(far == 2)
        def _():
            wave(3)

        @pl.when(far == 3)
        def _():
            for block in STEPS[NEAR:EARLY]:
                for which in range(3):
                    if (which, block) not in waited:
                        take(which, block)
            lax.fori_loop(NEAR, EARLY, near_row, 0)

        if EARLY > NEAR:
            @pl.when(far >= 3)
            def _():
                near_tile(NEAR, EARLY, far - 3)

        return carry

    lax.fori_loop(1, 7 if EARLY > NEAR else 5, near_chunk, 0)
    for block in STEPS[1:]:
        for which in range(3):
            if (which, block) not in waited:
                take(which, block)
    for step in range(1, GROUP):
        group_copy(step, inputs, group_x, x_send, x_recv).start()

    lax.fori_loop(NEAR, EARLY, near_out, 0)

    def row_block(index, carry):
        step = PLANE - 1 - index
        left, wide = row_operand(step)
        inner = jnp.concatenate([row_s[step], row_p[step]], axis=1)
        total = None
        block = 1024
        for start in range(0, WIDTH, block):
            p = col_p[...].reshape(WIDTH, PROBES)[start:start + block]
            part = tile(left, inner, start, block, p, mix[start:start + block, :])
            total = part if total is None else tuple(a + b for a, b in zip(total, part))
        finish_rows(step, *total, wide)
        return carry

    lax.fori_loop(0, PLANE - EARLY, row_block, 0)

    for step in range(1, GROUP):
        group_wait(step, inputs, group_x, x_send, x_recv)
    here = pl.multiple_of(member * SLICE, SLICE)

    def group_rows(pair, carry):
        rows = group_x[pl.ds(2 * pair, 2)].reshape(2 * ROWS, IN)
        start = pl.multiple_of(pair * 2 * ROWS, 2 * ROWS)
        group_xt[:, pl.ds(start, 2 * ROWS)] = rows.T
        pre = dot(rows, w_first[:, pl.ds(here, SLICE)])
        sigma = jax.nn.sigmoid(pre)
        factor[pl.ds(start, 2 * ROWS), :] = sigma * (1.0 + pre * (1.0 - sigma))
        return carry

    lax.fori_loop(0, GROUP // 2, group_rows, 0)

    def add_up(step, totals):
        for which in range(2):
            out_copy(step, which).wait_recv()
        return totals[0] + got_v[step].astype(f32), totals[1] + got_d[step].astype(f32)

    vsum, part = lax.fori_loop(1, PLANE, add_up, (out_v[0].astype(f32), out_d[0].astype(f32)))
    products[...] = (vsum * probe_gain).astype(bf16)
    lscale = loss_gain / math.sqrt(PROBES)
    length = inv_length[...]
    dfeat = part * (-lscale * jnp.concatenate([length, length], axis=1))
    packed_d = dfeat.astype(bf16)
    group_d[member] = packed_d
    for step in range(1, GROUP):
        group_copy(step, group_d.at[member], group_d, d_send, d_recv).start()

    second = dot(hidden_t[...], unpack_rows(packed_d))
    low = jnp.concatenate([second[: HID // 2], second[HID // 2:]], axis=1).astype(bf16)
    for far in range(4):
        tile = 8 * LANES + far
        chunks[:, tile * 8:tile * 8 + 8, :] = low[128 * far:128 * far + 128].reshape(PLANE, 8, 128)

    for step in range(1, GROUP):
        group_wait(step, group_d.at[member], group_d, d_send, d_recv)
    whole_d = jnp.concatenate([unpack_rows(group_d[item]) for item in range(GROUP)], axis=0)
    back = dot(whole_d, w_second[:, pl.ds(here, SLICE)])
    dpre = (back * factor[...]).astype(bf16)
    for far in range(8):
        first = dot(group_xt[128 * far:128 * far + 128, :], dpre).astype(bf16)
        for lane in range(LANES):
            tile = far * LANES + lane
            chunks[:, tile * 8:tile * 8 + 8, :] = first[:, 128 * lane:128 * lane + 128].reshape(PLANE, 8, 128)

    def place(px, py):
        return 2 * (4 * lax.rem(px, 2) + py) + lax.div(px, 2)

    def chunk_copy(step):
        px, py = plane_peer(step, 1)
        return remote(
            chunks.at[place(px, py)], got_chunks.at[step], chunk_send.at[step], chunk_recv.at[step],
            device(px, py, z, core),
        )

    def send_chunk(step, carry):
        chunk_copy(step).start()
        return carry

    lax.fori_loop(1, PLANE, send_chunk, 0)

    def add_chunk(step, total):
        chunk_copy(step).wait_recv()
        return total + got_chunks[step].astype(f32)

    summed = lax.fori_loop(1, PLANE, add_chunk, chunks[place(x, y)].astype(f32))

    depth = 8 * LANES
    for far in range(8):
        extra = 8 * depth + 8 * (far % 4)
        pieces[far] = jnp.concatenate(
            [summed[depth * far:depth * far + depth], summed[extra:extra + 8]], axis=0
        ).astype(bf16)

    own_slot = 2 * z + core

    def piece_copy(step):
        pz, pc = column_peer(step)
        return remote(
            pieces.at[pz], got_pieces.at[own_slot], piece_send.at[step], piece_recv.at[step],
            device(x, y, pz, pc),
        )

    def send_piece(step, carry):
        piece_copy(step).start()
        return carry

    lax.fori_loop(1, COLS, send_piece, 0)
    got_pieces[own_slot] = pieces[z]

    def wait_piece(step, carry):
        pz = lax.rem(z + 8 - lax.div(step, 2), 8)
        pc = lax.rem(core + lax.rem(step, 2), 2)
        remote(pieces.at[z], got_pieces.at[2 * pz + pc], piece_send.at[step], piece_recv.at[step], me).wait_recv()
        return carry

    lax.fori_loop(1, COLS, wait_piece, 0)
    strips = []
    tail = jnp.zeros((8, 128), f32)
    for item in range(GROUP):
        total = got_pieces[item].astype(f32)
        for other in range(item + GROUP, COLS, GROUP):
            total = total + got_pieces[other].astype(f32)
        strips += [total[8 * lane:8 * lane + 8] for lane in range(LANES)]
        tail = tail + total[depth:depth + 8]
    full = jnp.concatenate(strips, axis=1)
    grad_first[...] = jnp.where(core == 0, full[:4], full[4:])
    tail = jnp.where(z < 4, tail[:, :FEAT], tail[:, FEAT:])
    grad_second[...] = jnp.where(core == 0, tail[:4], tail[4:])

    for which in range(3):
        for far in range(4):
            up_copy(which, far).wait_send()
        for far in range(3):
            down_copy(which, far).wait_send()
        for slot in (0, 1, 4, 5, 8, 9, OWN, OWN + 2):
            side_copy(which, slot, 2).wait_send()

    def finish_plane(step, carry):
        for which in range(3):
            remote(
                rows[which].at[0], rows[which].at[step],
                row_send.at[which, step], row_recv.at[which, step], me,
            ).wait_send()
        for which in range(2):
            out_copy(step, which).wait_send()
        chunk_copy(step).wait_send()
        return carry

    lax.fori_loop(1, PLANE, finish_plane, 0)
    for step in range(1, GROUP):
        group_copy(step, inputs, group_x, x_send, x_recv).wait_send()
        group_copy(step, group_d.at[member], group_d, d_send, d_recv).wait_send()

    def finish_column(step, carry):
        piece_copy(step).wait_send()
        return carry

    lax.fori_loop(1, COLS, finish_column, 0)


def settle(products, grad_first, grad_second, out_products, out_first, out_second):
    out_products[...] = products[...]
    out_first[...] = grad_first[...]
    out_second[...] = grad_second[...]


def local(inputs, w_first, w_second, inv_length, probes, solves):
    vmem = pl.BlockSpec(memory_space=pltpu.VMEM)
    hbm = pl.BlockSpec(memory_space=pl.ANY)
    dma = pltpu.SemaphoreType.DMA
    shapes = (
        jax.ShapeDtypeStruct((ROWS, PROBES), bf16),
        jax.ShapeDtypeStruct((4, HID), f32),
        jax.ShapeDtypeStruct((4, FEAT), f32),
    )
    results = pl.pallas_call(
        kernel,
        out_shape=shapes,
        in_specs=[hbm, hbm, hbm, vmem, hbm, hbm],
        out_specs=(vmem, vmem, vmem),
        scratch_shapes=[
            pltpu.VMEM((IN, HID), bf16),
            pltpu.VMEM((FEAT, HID), bf16),
            pltpu.VMEM((PLANE, ROWS, PROBES), bf16),
            pltpu.VMEM((PLANE, ROWS, PROBES), bf16),
            pltpu.VMEM((PLANE, HALF, 2 * FEAT), bf16),
            pltpu.VMEM((COLS, ROWS, PROBES), bf16),
            pltpu.VMEM((COLS, ROWS, PROBES), bf16),
            pltpu.VMEM((COLS, HALF, 2 * FEAT), bf16),
            pltpu.VMEM((4 * FEAT, WIDTH), bf16),
            pltpu.VMEM((2 * PROBES, WIDTH), bf16),
            pltpu.VMEM((WIDTH, FEAT), bf16),
            pltpu.VMEM((EARLY * ROWS, 4 * FEAT), bf16),
            pltpu.VMEM((EARLY * ROWS, PROBES), f32),
            pltpu.VMEM((EARLY * ROWS, FEAT), f32),
            pltpu.VMEM((EARLY * ROWS, 128), f32),
            pltpu.VMEM((PLANE, ROWS, PROBES), bf16),
            pltpu.VMEM((PLANE, HALF, 2 * FEAT), bf16),
            pltpu.VMEM((PLANE, ROWS, PROBES), bf16),
            pltpu.VMEM((PLANE, HALF, 2 * FEAT), bf16),
            pltpu.VMEM((GROUP, ROWS, IN), bf16),
            pltpu.VMEM((IN, GROWS), bf16),
            pltpu.VMEM((GROWS, SLICE), f32),
            pltpu.VMEM((HID, ROWS), bf16),
            pltpu.VMEM((GROUP, HALF, 2 * FEAT), bf16),
            pltpu.VMEM((PLANE, TILES * 8, 128), bf16),
            pltpu.VMEM((PLANE, TILES * 8, 128), bf16),
            pltpu.VMEM((8, 8 * LANES + 8, 128), bf16),
            pltpu.VMEM((COLS, 8 * LANES + 8, 128), bf16),
            dma((7,)), dma((3, PLANE)), dma((3, PLANE)),
            dma((3, 4)), dma((3, 4)), dma((3, COLS)), dma((3, COLS)),
            dma((2, PLANE)), dma((2, PLANE)),
            dma((GROUP,)), dma((GROUP,)), dma((GROUP,)), dma((GROUP,)),
            dma((PLANE,)), dma((PLANE,)), dma((COLS,)), dma((COLS,)),
        ],
        compiler_params=pltpu.CompilerParams(
            collective_id=0, has_side_effects=True, vmem_limit_bytes=56 * 1024 * 1024
        ),
        name="gradient_step",
    )(inputs, w_first, w_second.T, inv_length.reshape(1, FEAT), probes, solves)
    return pl.pallas_call(
        settle, out_shape=shapes, in_specs=[vmem] * 3, out_specs=(vmem, vmem, vmem), name="settle"
    )(*results)


def solution(mesh):
    rows = P(("enc", "kr", "kc"), None)
    return jax.shard_map(
        local, mesh=mesh, in_specs=(rows, P(), P(), P(), rows, rows),
        out_specs=(rows, rows, rows), check_vma=False,
    )
```

```python
import functools
import math

import jax
import jax.numpy as jnp
from jax import lax
from jax.experimental import pallas as pl
from jax.experimental.pallas import tpu as pltpu
from jax.sharding import PartitionSpec as P

probe_gain = 0.5
loss_gain = 0.02

ROWS = 192
HALF = ROWS // 2
IN = 1024
HID = 1024
FEAT = 64
PROBES = 128
PLANE = 16
COLS = 16
WIDTH = COLS * ROWS
GROUP = 4
SLICE = HID // GROUP
GROWS = GROUP * ROWS
LANES = SLICE // 128
TILES = 8 * LANES + 4
LOG2E = 1.4426950408889634
MESH = pl.DeviceIdType.MESH
f32 = jnp.float32
bf16 = jnp.bfloat16


def dot(left, right):
    return jnp.dot(left, right, preferred_element_type=f32)


NEAR = 5
EARLY = 5
STEPS = (
    (0, 0), (0, 1), (0, 3), (1, 0), (3, 0), (1, 1), (3, 3), (1, 3),
    (3, 1), (0, 2), (2, 0), (2, 1), (2, 3), (1, 2), (3, 2), (2, 2),
)
PAIR = 2 * ROWS
CHUNK = 4 * ROWS
OWN = 12


def dot_nt(left, right):
    return lax.dot_general(left, right, (((1,), (1,)), ((), ())), preferred_element_type=f32)


def split3(value):
    one = value.astype(bf16)
    rest = value - one.astype(f32)
    two = rest.astype(bf16)
    three = (rest - two.astype(f32)).astype(bf16)
    return one, two, three


def unpack_rows(packed):
    return jnp.concatenate([packed[:, :FEAT], packed[:, FEAT:]], axis=0)


def pack_rows(value):
    half = value.shape[0] // 2
    return jnp.concatenate([value[:half], value[half:]], axis=1)


def half_norms(wide):
    return (-0.5 * LOG2E) * jnp.sum(wide * wide, axis=1, keepdims=True)


def extras(norms, own, other):
    one, two, three = split3(norms)
    lane = lax.broadcasted_iota(jnp.int32, (norms.shape[0], FEAT), 1)
    filled = jnp.where((lane >= other) & (lane < other + 3), 1.0, 0.0)
    filled = jnp.where(lane == own, one.astype(f32), filled)
    filled = jnp.where(lane == own + 1, two.astype(f32), filled)
    filled = jnp.where(lane == own + 2, three.astype(f32), filled)
    return filled.astype(bf16)


def kernel(
    inputs_hbm, w_first_hbm, w_second_hbm, inv_length, probes_hbm, solves_hbm,
    products, grad_first, grad_second,
    w_first, w_second, row_p, row_s, row_u, col_p, col_s, col_u, cross_t, inner_t, mix,
    left_near, left_next, near_v, near_m, near_s, out_v, out_d, got_v, got_d,
    group_x, group_xt, factor, hidden_t, group_d,
    chunks, got_chunks, pieces, got_pieces,
    load_sem, weight_sem, row_send, row_recv, up_send, down_send, side_send, col_recv,
    out_send, out_recv, x_send, x_recv, d_send, d_recv,
    chunk_send, chunk_recv, piece_send, piece_recv,
):
    z = lax.axis_index("enc")
    kr = lax.axis_index("kr")
    kc = lax.axis_index("kc")
    y = lax.rem(kr, 4)
    x = 2 * lax.div(kc, 2) + lax.div(kr, 4)
    core = lax.rem(kc, 2)

    def device(x, y, z, core):
        return (z, 4 * lax.rem(x, 2) + y, 2 * lax.div(x, 2) + core)

    def moved(dx, dy, sign):
        return lax.rem(x + 4 + sign * dx, 4), lax.rem(y + 4 + sign * dy, 4)

    def plane_peer(step, sign):
        return moved(lax.div(step, 4), lax.rem(step, 4), sign)

    def column_peer(step):
        return lax.rem(z + lax.div(step, 2), 8), lax.rem(core + lax.rem(step, 2), 2)

    def remote(src, dst, send, recv, target):
        return pltpu.make_async_remote_copy(
            src_ref=src, dst_ref=dst, send_sem=send, recv_sem=recv,
            device_id=target, device_id_type=MESH,
        )

    me = (z, kr, kc)
    sibling = device(x, y, z, 1 - core)
    up = device(x, y, lax.rem(z + 1, 8), core)
    down = device(x, y, lax.rem(z + 7, 8), core)
    z_low = lax.rem(z, 2)
    member = 2 * z_low + core

    barrier = pltpu.get_barrier_semaphore()

    loads = [
        pltpu.make_async_copy(source, target, load_sem.at[index])
        for index, (source, target) in enumerate((
            (inputs_hbm, group_x.at[member]), (w_second_hbm, w_second),
            (probes_hbm, col_p.at[OWN]), (solves_hbm, col_s.at[OWN]),
            (probes_hbm, row_p.at[0]), (solves_hbm, row_s.at[0]),
        ))
    ]

    def load_weights(block):
        here = pl.ds(pl.multiple_of(block * 256, 256), 256)
        return pltpu.make_async_copy(w_first_hbm.at[:, here], w_first.at[:, here], weight_sem.at[block])

    loads[0].start()
    for block in range(HID // 256):
        load_weights(block).start()
    for load in loads[1:]:
        load.start()

    def greet_plane(step, carry):
        px, py = plane_peer(step, 1)
        pl.semaphore_signal(barrier, inc=1, device_id=device(px, py, z, core), device_id_type=MESH)
        return carry

    def greet_column(step, carry):
        pz, pc = column_peer(step)
        pl.semaphore_signal(barrier, inc=1, device_id=device(x, y, pz, pc), device_id_type=MESH)
        return carry

    lax.fori_loop(1, PLANE, greet_plane, 0)
    lax.fori_loop(1, COLS, greet_column, 0)

    loads[0].wait()
    loads[1].wait()

    def encode(block, total):
        start = pl.multiple_of(block * 256, 256)
        load_weights(block).wait()
        pre = dot(group_x[member], w_first[:, pl.ds(start, 256)])
        hidden = (pre * jax.nn.sigmoid(pre)).astype(bf16)
        hidden_t[pl.ds(start, 256), :] = hidden.T
        return total + dot_nt(hidden, w_second[:, pl.ds(start, 256)])

    features = lax.fori_loop(0, HID // 256, encode, jnp.zeros((ROWS, FEAT), f32))
    scaled = (features * inv_length[...]).astype(bf16)
    packed = pack_rows(scaled)
    col_u[OWN] = packed
    row_u[0] = packed

    for load in loads[2:]:
        load.wait()

    pl.semaphore_wait(barrier, 30)

    columns = (col_u, col_p, col_s)
    rows = (row_u, row_p, row_s)

    def up_slot(far):
        if isinstance(far, int):
            return (OWN, 0, 4, 8, OWN + 2)[far]
        return jnp.where(far == 4, OWN + 2, 4 * far - 4)

    def down_slot(far):
        if isinstance(far, int):
            return (OWN, 1, 5, 9)[far]
        return 4 * far - 3

    def up_copy(which, far):
        buffer = columns[which]
        return remote(
            buffer.at[up_slot(far)], buffer.at[up_slot(far + 1)],
            up_send.at[which, far], col_recv.at[which, up_slot(far + 1)], up,
        )

    def down_copy(which, far):
        buffer = columns[which]
        return remote(
            buffer.at[down_slot(far)], buffer.at[down_slot(far + 1)],
            down_send.at[which, far], col_recv.at[which, down_slot(far + 1)], down,
        )

    def side_copy(which, slot, there):
        buffer = columns[which]
        return remote(
            buffer.at[slot], buffer.at[there], side_send.at[which, slot], col_recv.at[which, there], sibling,
        )

    def column_wait(which, slot):
        buffer = columns[which]
        remote(buffer.at[slot], buffer.at[slot], side_send.at[which, 0], col_recv.at[which, slot], me).wait_recv()

    def row_send_on(which, source, dx, dy, here):
        slot = STEPS.index(here)
        px, py = moved(dx, dy, 1)
        return remote(
            rows[which].at[STEPS.index(source)], rows[which].at[slot],
            row_send.at[which, slot], row_recv.at[which, slot], device(px, py, z, core),
        )

    def row_wait(which, step):
        remote(
            rows[which].at[0], rows[which].at[step],
            row_send.at[which, step], row_recv.at[which, step], me,
        ).wait_recv()

    ways = ((1, 3), (1, 1), (0, 3))

    def offset(axis, along, across):
        return (along, across) if axis == 0 else (across, along)

    def spread(which, block):
        first, turn = ways[which]
        second = 1 - first
        along, across = block[first], block[second]
        moves = []
        if across == 0:
            if along == 0:
                moves += [(first, 1), (first, 3)]
            elif along == (4 - turn) % 4:
                moves.append((first, turn))
            moves += [(second, 1), (second, 3)]
        elif across == (4 - turn) % 4:
            moves.append((second, turn))
        for axis, way in moves:
            here = [block[0], block[1]]
            here[axis] = (here[axis] - way) % 4
            row_send_on(which, block, *offset(axis, way, 0), tuple(here)).start()

    waited = set()

    def take(which, block):
        waited.add((which, block))
        row_wait(which, STEPS.index(block))
        spread(which, block)

    def wave(level, items=(0, 1, 2)):
        for which in items:
            for block in STEPS[1:]:
                first, turn = ways[which]
                far = [0 if item == 0 else 2 if item == 2 else 1 for item in block]
                goes_on = block[1 - first] == 0 or block[1 - first] == (4 - turn) % 4
                if sum(far) == level and goes_on:
                    take(which, block)

    for which in range(3):
        up_copy(which, 0).start()
        down_copy(which, 0).start()
        spread(which, (0, 0))
        side_copy(which, OWN, OWN + 1).start()

    def advance(far, items=(0, 1, 2)):
        for which in items:
            here = up_slot(far)
            column_wait(which, here)

            @pl.when(far < 4)
            def _():
                up_copy(which, far).start()

            side_copy(which, here, jnp.where(far == 4, OWN + 3, 4 * far - 2)).start()

            @pl.when(far < 4)
            def _():
                column_wait(which, down_slot(far))

                @pl.when(far < 3)
                def _():
                    down_copy(which, far).start()

                side_copy(which, down_slot(far), 4 * far - 1).start()

    def group_copy(step, source, buffer, send, recv):
        other = lax.rem(member + step, GROUP)
        pz = z - z_low + lax.div(other, 2)
        return remote(source, buffer.at[member], send.at[step], recv.at[step], device(x, y, pz, lax.rem(other, 2)))

    def group_wait(step, source, buffer, send, recv):
        other = lax.rem(member + GROUP - step, GROUP)
        remote(source, buffer.at[other], send.at[step], recv.at[step], me).wait_recv()

    inputs = group_x.at[member]

    def row_operand(step):
        wide = unpack_rows(row_u[step]).astype(f32)
        u = wide.astype(bf16)
        return jnp.concatenate([u, u, u, extras(half_norms(wide), 0, 3)], axis=1), wide

    near_v[...] = jnp.zeros_like(near_v)
    near_m[...] = jnp.zeros_like(near_m)
    near_s[...] = jnp.zeros_like(near_s)
    def near_row(step, carry):
        left_near[pl.ds(pl.multiple_of(step * ROWS, ROWS), ROWS), :] = row_operand(step)[0]
        return carry

    for items in ((0,), (1, 2)):
        advance(1, items)
        wave(1, items)
        for block in STEPS[1:NEAR]:
            for which in items:
                if (which, block) not in waited:
                    take(which, block)
        if 0 in items:
            lax.fori_loop(0, NEAR, near_row, 0)

    def prepare(pair):
        slot = 2 * pair
        start = pl.multiple_of(slot * ROWS, PAIR)
        u = jnp.concatenate([unpack_rows(col_u[slot]), unpack_rows(col_u[slot + 1])], axis=0)
        wide = u.astype(f32)
        one, two, three = split3(wide * LOG2E)
        tail = extras(half_norms(wide), 3, 0)
        operand = jnp.concatenate([one, two, three, tail], axis=1)
        cross_t[:, pl.ds(start, PAIR)] = operand.T
        p = jnp.concatenate([col_p[slot], col_p[slot + 1]], axis=0)
        s = jnp.concatenate([col_s[slot], col_s[slot + 1]], axis=0)
        inner_t[pl.ds(0, PROBES), pl.ds(start, PAIR)] = p.T
        inner_t[pl.ds(PROBES, PROBES), pl.ds(start, PAIR)] = s.T
        mix[pl.ds(start, PAIR), :] = u

    def tile(left, inner, start, size, p, u):
        value = jnp.exp2(dot(left, cross_t[:, pl.ds(start, size)]))
        both = value * dot(inner, inner_t[:, pl.ds(start, size)])
        sums = both[:, :128]
        for lane in range(128, size, 128):
            sums = sums + both[:, lane:lane + 128]
        return dot(value.astype(bf16), p), dot(both.astype(bf16), u), sums

    def near_tile(low, high, chunk):
        size = (high - low) * ROWS
        here = pl.ds(low * ROWS, size)
        start = pl.multiple_of(chunk * CHUNK, CHUNK)
        inner = jnp.concatenate(
            [row_s[low:high].reshape(size, PROBES), row_p[low:high].reshape(size, PROBES)], axis=1
        )
        p = col_p[pl.ds(4 * chunk, 4)].reshape(CHUNK, PROBES)
        vsum, mixed, sums = tile(left_near[here, :], inner, start, CHUNK, p, mix[pl.ds(start, CHUNK), :])
        near_v[here, :] += vsum
        near_m[here, :] += mixed
        near_s[here, :] += sums

    def table(step, values):
        if isinstance(step, int):
            return values[step]
        total = 0
        for index, value in enumerate(values):
            if value:
                total = total + jnp.where(step == index, value, 0)
        return total

    def out_copy(step, which):
        dx = table(step, [item[0] for item in STEPS])
        dy = table(step, [item[1] for item in STEPS])
        px, py = moved(dx, dy, 1)
        source = (out_v, out_d)[which]
        target = (got_v, got_d)[which]
        return remote(
            source.at[step], target.at[step], out_send.at[which, step], out_recv.at[which, step],
            device(px, py, z, core),
        )

    def finish_rows(step, vsum, mixed, sums, wide):
        part = jnp.sum(sums, axis=1, keepdims=True) * wide - mixed
        out_v[step] = vsum.astype(bf16)
        out_d[step] = pack_rows(part).astype(bf16)

        @pl.when(step > 0)
        def _():
            out_copy(step, 0).start()
            out_copy(step, 1).start()

    def near_out(step, carry):
        here = pl.ds(pl.multiple_of(step * ROWS, ROWS), ROWS)
        wide = unpack_rows(row_u[step]).astype(f32)
        finish_rows(step, near_v[here, :], near_m[here, :], near_s[here, :], wide)
        return carry

    def near_chunk(far, carry):
        @pl.when(far <= 4)
        def _():
            for which in range(3):
                @pl.when(far < 4)
                def _():
                    column_wait(which, 4 * far - 2)
                    column_wait(which, 4 * far - 1)

                @pl.when(far == 4)
                def _():
                    column_wait(which, OWN + 1)
                    column_wait(which, OWN + 3)

            prepare(2 * far - 2)
            prepare(2 * far - 1)
            near_tile(0, NEAR, far - 1)

        @pl.when(far == 4)
        def _():
            lax.fori_loop(0, NEAR, near_out, 0)

        @pl.when(far < 4)
        def _():
            advance(far + 1)

        @pl.when(far == 1)
        def _():
            wave(2)

        @pl.when(far == 2)
        def _():
            wave(3)

        @pl.when(far == 3)
        def _():
            for block in STEPS[NEAR:EARLY]:
                for which in range(3):
                    if (which, block) not in waited:
                        take(which, block)
            lax.fori_loop(NEAR, EARLY, near_row, 0)

        if EARLY > NEAR:
            @pl.when(far >= 3)
            def _():
                near_tile(NEAR, EARLY, far - 3)

        return carry

    lax.fori_loop(1, 7 if EARLY > NEAR else 5, near_chunk, 0)
    for block in STEPS[1:]:
        for which in range(3):
            if (which, block) not in waited:
                take(which, block)
    for step in range(1, GROUP):
        group_copy(step, inputs, group_x, x_send, x_recv).start()

    lax.fori_loop(NEAR, EARLY, near_out, 0)

    def row_block(index, carry):
        step = PLANE - 1 - index
        wide = unpack_rows(row_u[step]).astype(f32)
        left = left_next[lax.rem(index, 2)]
        left_next[lax.rem(index + 1, 2)] = row_operand(jnp.maximum(step - 1, NEAR))[0]
        inner = jnp.concatenate([row_s[step], row_p[step]], axis=1)
        total = None
        block = 1024
        for start in range(0, WIDTH, block):
            p = col_p[...].reshape(WIDTH, PROBES)[start:start + block]
            part = tile(left, inner, start, block, p, mix[start:start + block, :])
            total = part if total is None else tuple(a + b for a, b in zip(total, part))
        finish_rows(step, *total, wide)
        return carry

    left_next[0] = row_operand(PLANE - 1)[0]
    lax.fori_loop(0, PLANE - EARLY, row_block, 0)

    for step in range(1, GROUP):
        group_wait(step, inputs, group_x, x_send, x_recv)
    here = pl.multiple_of(member * SLICE, SLICE)

    def group_rows(pair, carry):
        rows = group_x[pl.ds(2 * pair, 2)].reshape(2 * ROWS, IN)
        start = pl.multiple_of(pair * 2 * ROWS, 2 * ROWS)
        group_xt[:, pl.ds(start, 2 * ROWS)] = rows.T
        pre = dot(rows, w_first[:, pl.ds(here, SLICE)])
        sigma = jax.nn.sigmoid(pre)
        factor[pl.ds(start, 2 * ROWS), :] = sigma * (1.0 + pre * (1.0 - sigma))
        return carry

    lax.fori_loop(0, GROUP // 2, group_rows, 0)

    def add_up(step, totals):
        for which in range(2):
            out_copy(step, which).wait_recv()
        return totals[0] + got_v[step].astype(f32), totals[1] + got_d[step].astype(f32)

    vsum, part = lax.fori_loop(1, PLANE, add_up, (out_v[0].astype(f32), out_d[0].astype(f32)))
    products[...] = (vsum * probe_gain).astype(bf16)
    lscale = loss_gain / math.sqrt(PROBES)
    length = inv_length[...]
    dfeat = part * (-lscale * jnp.concatenate([length, length], axis=1))
    packed_d = dfeat.astype(bf16)
    group_d[member] = packed_d
    for step in range(1, GROUP):
        group_copy(step, group_d.at[member], group_d, d_send, d_recv).start()

    def place(px, py):
        return 2 * (4 * lax.rem(px, 2) + py) + lax.div(px, 2)

    def chunk_copy(step, part):
        px, py = plane_peer(step, 1)
        here = (pl.ds(0, 64 * LANES), pl.ds(64 * LANES, 32))[part]
        return remote(
            chunks.at[place(px, py), here], got_chunks.at[step, here],
            chunk_send.at[part, step], chunk_recv.at[part, step], device(px, py, z, core),
        )

    def send_chunk(part):
        def send(step, carry):
            chunk_copy(step, part).start()
            return carry

        return send

    second = dot(hidden_t[...], unpack_rows(packed_d))
    low = jnp.concatenate([second[: HID // 2], second[HID // 2:]], axis=1).astype(bf16)
    for far in range(4):
        tile = 8 * LANES + far
        chunks[:, tile * 8:tile * 8 + 8, :] = low[128 * far:128 * far + 128].reshape(PLANE, 8, 128)

    lax.fori_loop(1, PLANE, send_chunk(1), 0)
    for step in range(1, GROUP):
        group_wait(step, group_d.at[member], group_d, d_send, d_recv)
    whole_d = jnp.concatenate([unpack_rows(group_d[item]) for item in range(GROUP)], axis=0)
    back = dot(whole_d, w_second[:, pl.ds(here, SLICE)])
    dpre = (back * factor[...]).astype(bf16)
    for far in range(8):
        first = dot(group_xt[128 * far:128 * far + 128, :], dpre).astype(bf16)
        for lane in range(LANES):
            tile = far * LANES + lane
            chunks[:, tile * 8:tile * 8 + 8, :] = first[:, 128 * lane:128 * lane + 128].reshape(PLANE, 8, 128)

    lax.fori_loop(1, PLANE, send_chunk(0), 0)

    def add_chunk(step, total):
        chunk_copy(step, 1).wait_recv()
        chunk_copy(step, 0).wait_recv()
        return total + got_chunks[step].astype(f32)

    summed = lax.fori_loop(1, PLANE, add_chunk, chunks[place(x, y)].astype(f32))

    depth = 8 * LANES
    for far in range(8):
        extra = 8 * depth + 8 * (far % 4)
        pieces[far] = jnp.concatenate(
            [summed[depth * far:depth * far + depth], summed[extra:extra + 8]], axis=0
        ).astype(bf16)

    own_slot = 2 * z + core

    def piece_copy(step):
        pz, pc = column_peer(step)
        return remote(
            pieces.at[pz], got_pieces.at[own_slot], piece_send.at[step], piece_recv.at[step],
            device(x, y, pz, pc),
        )

    def send_piece(step, carry):
        piece_copy(step).start()
        return carry

    lax.fori_loop(1, COLS, send_piece, 0)
    got_pieces[own_slot] = pieces[z]

    def wait_piece(step, carry):
        pz = lax.rem(z + 8 - lax.div(step, 2), 8)
        pc = lax.rem(core + lax.rem(step, 2), 2)
        remote(pieces.at[z], got_pieces.at[2 * pz + pc], piece_send.at[step], piece_recv.at[step], me).wait_recv()
        return carry

    lax.fori_loop(1, COLS, wait_piece, 0)
    strips = []
    tail = jnp.zeros((8, 128), f32)
    for item in range(GROUP):
        total = got_pieces[item].astype(f32)
        for other in range(item + GROUP, COLS, GROUP):
            total = total + got_pieces[other].astype(f32)
        strips += [total[8 * lane:8 * lane + 8] for lane in range(LANES)]
        tail = tail + total[depth:depth + 8]
    full = jnp.concatenate(strips, axis=1)
    grad_first[...] = jnp.where(core == 0, full[:4], full[4:])
    tail = jnp.where(z < 4, tail[:, :FEAT], tail[:, FEAT:])
    grad_second[...] = jnp.where(core == 0, tail[:4], tail[4:])

    for which in range(3):
        for far in range(4):
            up_copy(which, far).wait_send()
        for far in range(3):
            down_copy(which, far).wait_send()
        for slot in (0, 1, 4, 5, 8, 9, OWN, OWN + 2):
            side_copy(which, slot, 2).wait_send()

    def finish_plane(step, carry):
        for which in range(3):
            remote(
                rows[which].at[0], rows[which].at[step],
                row_send.at[which, step], row_recv.at[which, step], me,
            ).wait_send()
        for which in range(2):
            out_copy(step, which).wait_send()
        chunk_copy(step, 0).wait_send()
        chunk_copy(step, 1).wait_send()
        return carry

    lax.fori_loop(1, PLANE, finish_plane, 0)
    for step in range(1, GROUP):
        group_copy(step, inputs, group_x, x_send, x_recv).wait_send()
        group_copy(step, group_d.at[member], group_d, d_send, d_recv).wait_send()

    def finish_column(step, carry):
        piece_copy(step).wait_send()
        return carry

    lax.fori_loop(1, COLS, finish_column, 0)


def settle(products, grad_first, grad_second, out_products, out_first, out_second):
    out_products[...] = products[...]
    out_first[...] = grad_first[...]
    out_second[...] = grad_second[...]


def local(inputs, w_first, w_second, inv_length, probes, solves):
    vmem = pl.BlockSpec(memory_space=pltpu.VMEM)
    hbm = pl.BlockSpec(memory_space=pl.ANY)
    dma = pltpu.SemaphoreType.DMA
    shapes = (
        jax.ShapeDtypeStruct((ROWS, PROBES), bf16),
        jax.ShapeDtypeStruct((4, HID), f32),
        jax.ShapeDtypeStruct((4, FEAT), f32),
    )
    results = pl.pallas_call(
        kernel,
        out_shape=shapes,
        in_specs=[hbm, hbm, hbm, vmem, hbm, hbm],
        out_specs=(vmem, vmem, vmem),
        scratch_shapes=[
            pltpu.VMEM((IN, HID), bf16),
            pltpu.VMEM((FEAT, HID), bf16),
            pltpu.VMEM((PLANE, ROWS, PROBES), bf16),
            pltpu.VMEM((PLANE, ROWS, PROBES), bf16),
            pltpu.VMEM((PLANE, HALF, 2 * FEAT), bf16),
            pltpu.VMEM((COLS, ROWS, PROBES), bf16),
            pltpu.VMEM((COLS, ROWS, PROBES), bf16),
            pltpu.VMEM((COLS, HALF, 2 * FEAT), bf16),
            pltpu.VMEM((4 * FEAT, WIDTH), bf16),
            pltpu.VMEM((2 * PROBES, WIDTH), bf16),
            pltpu.VMEM((WIDTH, FEAT), bf16),
            pltpu.VMEM((EARLY * ROWS, 4 * FEAT), bf16),
            pltpu.VMEM((2, ROWS, 4 * FEAT), bf16),
            pltpu.VMEM((EARLY * ROWS, PROBES), f32),
            pltpu.VMEM((EARLY * ROWS, FEAT), f32),
            pltpu.VMEM((EARLY * ROWS, 128), f32),
            pltpu.VMEM((PLANE, ROWS, PROBES), bf16),
            pltpu.VMEM((PLANE, HALF, 2 * FEAT), bf16),
            pltpu.VMEM((PLANE, ROWS, PROBES), bf16),
            pltpu.VMEM((PLANE, HALF, 2 * FEAT), bf16),
            pltpu.VMEM((GROUP, ROWS, IN), bf16),
            pltpu.VMEM((IN, GROWS), bf16),
            pltpu.VMEM((GROWS, SLICE), f32),
            pltpu.VMEM((HID, ROWS), bf16),
            pltpu.VMEM((GROUP, HALF, 2 * FEAT), bf16),
            pltpu.VMEM((PLANE, TILES * 8, 128), bf16),
            pltpu.VMEM((PLANE, TILES * 8, 128), bf16),
            pltpu.VMEM((8, 8 * LANES + 8, 128), bf16),
            pltpu.VMEM((COLS, 8 * LANES + 8, 128), bf16),
            dma((6,)), dma((HID // 256,)), dma((3, PLANE)), dma((3, PLANE)),
            dma((3, 4)), dma((3, 4)), dma((3, COLS)), dma((3, COLS)),
            dma((2, PLANE)), dma((2, PLANE)),
            dma((GROUP,)), dma((GROUP,)), dma((GROUP,)), dma((GROUP,)),
            dma((2, PLANE)), dma((2, PLANE)), dma((COLS,)), dma((COLS,)),
        ],
        compiler_params=pltpu.CompilerParams(
            collective_id=0, has_side_effects=True, vmem_limit_bytes=56 * 1024 * 1024
        ),
        name="gradient_step",
    )(inputs, w_first, w_second.T, inv_length.reshape(1, FEAT), probes, solves)
    return pl.pallas_call(
        settle, out_shape=shapes, in_specs=[vmem] * 3, out_specs=(vmem, vmem, vmem), name="settle"
    )(*results)


def solution(mesh):
    rows = P(("enc", "kr", "kc"), None)
    return jax.shard_map(
        local, mesh=mesh, in_specs=(rows, P(), P(), P(), rows, rows),
        out_specs=(rows, rows, rows), check_vma=False,
    )
```

```python
import functools
import math

import jax
import jax.numpy as jnp
from jax import lax
from jax.experimental import pallas as pl
from jax.experimental.pallas import tpu as pltpu
from jax.sharding import PartitionSpec as P

probe_gain = 0.5
loss_gain = 0.02

ROWS = 192
HALF = ROWS // 2
IN = 1024
HID = 1024
FEAT = 64
PROBES = 128
PLANE = 16
COLS = 16
WIDTH = COLS * ROWS
GROUP = 4
SLICE = HID // GROUP
GROWS = GROUP * ROWS
LANES = SLICE // 128
TILES = 8 * LANES + 4
LOG2E = 1.4426950408889634
MESH = pl.DeviceIdType.MESH
f32 = jnp.float32
bf16 = jnp.bfloat16


def dot(left, right):
    return jnp.dot(left, right, preferred_element_type=f32)


NEAR = 5
EARLY = 5
STEPS = (
    (0, 0), (0, 1), (0, 3), (1, 0), (3, 0), (1, 1), (3, 3), (1, 3),
    (3, 1), (0, 2), (2, 0), (2, 1), (2, 3), (1, 2), (3, 2), (2, 2),
)
PAIR = 2 * ROWS
CHUNK = 4 * ROWS
OWN = 2


def dot_nt(left, right):
    return lax.dot_general(left, right, (((1,), (1,)), ((), ())), preferred_element_type=f32)


def split3(value):
    one = value.astype(bf16)
    rest = value - one.astype(f32)
    two = rest.astype(bf16)
    three = (rest - two.astype(f32)).astype(bf16)
    return one, two, three


def unpack_rows(packed):
    return jnp.concatenate([packed[:, :FEAT], packed[:, FEAT:]], axis=0)


def pack_rows(value):
    half = value.shape[0] // 2
    return jnp.concatenate([value[:half], value[half:]], axis=1)


def half_norms(wide):
    return (-0.5 * LOG2E) * jnp.sum(wide * wide, axis=1, keepdims=True)


def extras(norms, own, other):
    one, two, three = split3(norms)
    lane = lax.broadcasted_iota(jnp.int32, (norms.shape[0], FEAT), 1)
    filled = jnp.where((lane >= other) & (lane < other + 3), 1.0, 0.0)
    filled = jnp.where(lane == own, one.astype(f32), filled)
    filled = jnp.where(lane == own + 1, two.astype(f32), filled)
    filled = jnp.where(lane == own + 2, three.astype(f32), filled)
    return filled.astype(bf16)


def kernel(
    inputs_hbm, w_first_hbm, w_second_hbm, inv_length, probes_hbm, solves_hbm,
    products, grad_first, grad_second,
    w_first, w_second, row_p, row_s, row_u, col_p, col_s, col_u, cross_t, inner_t, mix,
    left_near, left_next, near_v, near_m, near_s, out_v, out_d, got_v, got_d,
    group_x, group_xt, factor, hidden_t, group_d,
    chunks, got_chunks, pieces, got_pieces,
    load_sem, weight_sem, row_send, row_recv, up_send, down_send, side_send, col_recv,
    out_send, out_recv, x_send, x_recv, d_send, d_recv,
    chunk_send, chunk_recv, piece_send, piece_recv,
):
    z = lax.axis_index("enc")
    kr = lax.axis_index("kr")
    kc = lax.axis_index("kc")
    y = lax.rem(kr, 4)
    x = 2 * lax.div(kc, 2) + lax.div(kr, 4)
    core = lax.rem(kc, 2)

    def device(x, y, z, core):
        return (z, 4 * lax.rem(x, 2) + y, 2 * lax.div(x, 2) + core)

    def moved(dx, dy, sign):
        return lax.rem(x + 4 + sign * dx, 4), lax.rem(y + 4 + sign * dy, 4)

    def plane_peer(step, sign):
        return moved(lax.div(step, 4), lax.rem(step, 4), sign)

    def column_peer(step):
        return lax.rem(z + lax.div(step, 2), 8), lax.rem(core + lax.rem(step, 2), 2)

    def remote(src, dst, send, recv, target):
        return pltpu.make_async_remote_copy(
            src_ref=src, dst_ref=dst, send_sem=send, recv_sem=recv,
            device_id=target, device_id_type=MESH,
        )

    me = (z, kr, kc)
    sibling = device(x, y, z, 1 - core)
    up = device(x, y, lax.rem(z + 1, 8), core)
    down = device(x, y, lax.rem(z + 7, 8), core)
    z_low = lax.rem(z, 2)
    member = 2 * z_low + core

    barrier = pltpu.get_barrier_semaphore()

    loads = [
        pltpu.make_async_copy(source, target, load_sem.at[index])
        for index, (source, target) in enumerate((
            (inputs_hbm, group_x.at[member]), (w_second_hbm, w_second),
            (probes_hbm, col_p.at[OWN]), (solves_hbm, col_s.at[OWN]),
            (probes_hbm, row_p.at[0]), (solves_hbm, row_s.at[0]),
        ))
    ]

    def load_weights(block):
        here = pl.ds(pl.multiple_of(block * 256, 256), 256)
        return pltpu.make_async_copy(w_first_hbm.at[:, here], w_first.at[:, here], weight_sem.at[block])

    loads[0].start()
    for block in range(HID // 256):
        load_weights(block).start()
    for load in loads[1:]:
        load.start()

    def greet_plane(step, carry):
        px, py = plane_peer(step, 1)
        pl.semaphore_signal(barrier, inc=1, device_id=device(px, py, z, core), device_id_type=MESH)
        return carry

    def greet_column(step, carry):
        pz, pc = column_peer(step)
        pl.semaphore_signal(barrier, inc=1, device_id=device(x, y, pz, pc), device_id_type=MESH)
        return carry

    lax.fori_loop(1, PLANE, greet_plane, 0)
    lax.fori_loop(1, COLS, greet_column, 0)

    loads[0].wait()
    loads[1].wait()

    def encode(block, total):
        start = pl.multiple_of(block * 256, 256)
        load_weights(block).wait()
        pre = dot(group_x[member], w_first[:, pl.ds(start, 256)])
        hidden = (pre * jax.nn.sigmoid(pre)).astype(bf16)
        hidden_t[pl.ds(start, 256), :] = hidden.T
        return total + dot_nt(hidden, w_second[:, pl.ds(start, 256)])

    features = lax.fori_loop(0, HID // 256, encode, jnp.zeros((ROWS, FEAT), f32))
    scaled = (features * inv_length[...]).astype(bf16)
    packed = pack_rows(scaled)
    col_u[OWN] = packed
    row_u[0] = packed

    for load in loads[2:]:
        load.wait()

    pl.semaphore_wait(barrier, 30)

    columns = (col_u, col_p, col_s)
    rows = (row_u, row_p, row_s)

    def up_slot(far):
        if isinstance(far, int):
            return (OWN, 0, 4, 8, 12)[far]
        return 4 * far - 4

    def down_slot(far):
        if isinstance(far, int):
            return (OWN, 1, 5, 9)[far]
        return 4 * far - 3

    def up_copy(which, far):
        buffer = columns[which]
        return remote(
            buffer.at[up_slot(far)], buffer.at[up_slot(far + 1)],
            up_send.at[which, far], col_recv.at[which, up_slot(far + 1)], up,
        )

    def down_copy(which, far):
        buffer = columns[which]
        return remote(
            buffer.at[down_slot(far)], buffer.at[down_slot(far + 1)],
            down_send.at[which, far], col_recv.at[which, down_slot(far + 1)], down,
        )

    def side_copy(which, slot, there):
        buffer = columns[which]
        return remote(
            buffer.at[slot], buffer.at[there], side_send.at[which, slot], col_recv.at[which, there], sibling,
        )

    def column_wait(which, slot):
        buffer = columns[which]
        remote(buffer.at[slot], buffer.at[slot], side_send.at[which, 0], col_recv.at[which, slot], me).wait_recv()

    def row_send_on(which, source, dx, dy, here):
        slot = STEPS.index(here)
        px, py = moved(dx, dy, 1)
        return remote(
            rows[which].at[STEPS.index(source)], rows[which].at[slot],
            row_send.at[which, slot], row_recv.at[which, slot], device(px, py, z, core),
        )

    def row_wait(which, step):
        remote(
            rows[which].at[0], rows[which].at[step],
            row_send.at[which, step], row_recv.at[which, step], me,
        ).wait_recv()

    ways = ((1, 3), (1, 1), (0, 3))

    def offset(axis, along, across):
        return (along, across) if axis == 0 else (across, along)

    def spread(which, block):
        first, turn = ways[which]
        second = 1 - first
        along, across = block[first], block[second]
        moves = []
        if across == 0:
            if along == 0:
                moves += [(first, 1), (first, 3)]
            elif along == (4 - turn) % 4:
                moves.append((first, turn))
            moves += [(second, 1), (second, 3)]
        elif across == (4 - turn) % 4:
            moves.append((second, turn))
        for axis, way in moves:
            here = [block[0], block[1]]
            here[axis] = (here[axis] - way) % 4
            row_send_on(which, block, *offset(axis, way, 0), tuple(here)).start()

    waited = set()

    def take(which, block):
        waited.add((which, block))
        row_wait(which, STEPS.index(block))
        spread(which, block)

    def wave(level, items=(0, 1, 2)):
        for which in items:
            for block in STEPS[1:]:
                first, turn = ways[which]
                far = [0 if item == 0 else 2 if item == 2 else 1 for item in block]
                goes_on = block[1 - first] == 0 or block[1 - first] == (4 - turn) % 4
                if sum(far) == level and goes_on:
                    take(which, block)

    for which in range(3):
        up_copy(which, 0).start()
        down_copy(which, 0).start()
        spread(which, (0, 0))
        side_copy(which, OWN, OWN + 1).start()

    def advance(far, items=(0, 1, 2)):
        for which in items:
            here = up_slot(far)
            column_wait(which, here)

            @pl.when(far < 4)
            def _():
                up_copy(which, far).start()

            side_copy(which, here, jnp.where(far == 4, 13, 4 * far + 2)).start()

            @pl.when(far < 4)
            def _():
                column_wait(which, down_slot(far))

                @pl.when(far < 3)
                def _():
                    down_copy(which, far).start()

                side_copy(which, down_slot(far), 4 * far + 3).start()

    def group_copy(step, source, buffer, send, recv):
        other = lax.rem(member + step, GROUP)
        pz = z - z_low + lax.div(other, 2)
        return remote(source, buffer.at[member], send.at[step], recv.at[step], device(x, y, pz, lax.rem(other, 2)))

    def group_wait(step, source, buffer, send, recv):
        other = lax.rem(member + GROUP - step, GROUP)
        remote(source, buffer.at[other], send.at[step], recv.at[step], me).wait_recv()

    inputs = group_x.at[member]

    def row_operand(step):
        wide = unpack_rows(row_u[step]).astype(f32)
        u = wide.astype(bf16)
        return jnp.concatenate([u, u, u, extras(half_norms(wide), 0, 3)], axis=1), wide

    near_v[...] = jnp.zeros_like(near_v)
    near_m[...] = jnp.zeros_like(near_m)
    near_s[...] = jnp.zeros_like(near_s)
    def near_row(step, carry):
        left_near[pl.ds(pl.multiple_of(step * ROWS, ROWS), ROWS), :] = row_operand(step)[0]
        return carry

    for items in ((0,), (1, 2)):
        advance(1, items)
        wave(1, items)
        for block in STEPS[1:NEAR]:
            for which in items:
                if (which, block) not in waited:
                    take(which, block)
        if 0 in items:
            lax.fori_loop(0, NEAR, near_row, 0)

    def prepare(pair):
        slot = 2 * pair
        start = pl.multiple_of(slot * ROWS, PAIR)
        u = jnp.concatenate([unpack_rows(col_u[slot]), unpack_rows(col_u[slot + 1])], axis=0)
        wide = u.astype(f32)
        one, two, three = split3(wide * LOG2E)
        tail = extras(half_norms(wide), 3, 0)
        operand = jnp.concatenate([one, two, three, tail], axis=1)
        cross_t[:, pl.ds(start, PAIR)] = operand.T
        p = jnp.concatenate([col_p[slot], col_p[slot + 1]], axis=0)
        s = jnp.concatenate([col_s[slot], col_s[slot + 1]], axis=0)
        inner_t[pl.ds(0, PROBES), pl.ds(start, PAIR)] = p.T
        inner_t[pl.ds(PROBES, PROBES), pl.ds(start, PAIR)] = s.T
        mix[pl.ds(start, PAIR), :] = u

    def tile(left, inner, start, size, p, u):
        value = jnp.exp2(dot(left, cross_t[:, pl.ds(start, size)]))
        both = value * dot(inner, inner_t[:, pl.ds(start, size)])
        sums = both[:, :128]
        for lane in range(128, size, 128):
            sums = sums + both[:, lane:lane + 128]
        return dot(value.astype(bf16), p), dot(both.astype(bf16), u), sums

    def near_tile(low, high, chunk):
        size = (high - low) * ROWS
        here = pl.ds(low * ROWS, size)
        start = pl.multiple_of(chunk * CHUNK, CHUNK)
        inner = jnp.concatenate(
            [row_s[low:high].reshape(size, PROBES), row_p[low:high].reshape(size, PROBES)], axis=1
        )
        p = col_p[pl.ds(4 * chunk, 4)].reshape(CHUNK, PROBES)
        vsum, mixed, sums = tile(left_near[here, :], inner, start, CHUNK, p, mix[pl.ds(start, CHUNK), :])
        near_v[here, :] += vsum
        near_m[here, :] += mixed
        near_s[here, :] += sums

    def table(step, values):
        if isinstance(step, int):
            return values[step]
        total = 0
        for index, value in enumerate(values):
            if value:
                total = total + jnp.where(step == index, value, 0)
        return total

    def out_copy(step, which):
        dx = table(step, [item[0] for item in STEPS])
        dy = table(step, [item[1] for item in STEPS])
        px, py = moved(dx, dy, 1)
        source = (out_v, out_d)[which]
        target = (got_v, got_d)[which]
        return remote(
            source.at[step], target.at[step], out_send.at[which, step], out_recv.at[which, step],
            device(px, py, z, core),
        )

    def finish_rows(step, vsum, mixed, sums, wide):
        part = jnp.sum(sums, axis=1, keepdims=True) * wide - mixed
        out_v[step] = vsum.astype(bf16)
        out_d[step] = pack_rows(part).astype(bf16)

        @pl.when(step > 0)
        def _():
            out_copy(step, 0).start()
            out_copy(step, 1).start()

    def near_out(step, carry):
        here = pl.ds(pl.multiple_of(step * ROWS, ROWS), ROWS)
        wide = unpack_rows(row_u[step]).astype(f32)
        finish_rows(step, near_v[here, :], near_m[here, :], near_s[here, :], wide)
        return carry

    def near_chunk(far, carry):
        @pl.when(far <= 4)
        def _():
            for which in range(3):
                @pl.when(far == 1)
                def _():
                    column_wait(which, OWN + 1)

                @pl.when(far > 1)
                def _():
                    column_wait(which, 4 * far - 2)
                    column_wait(which, 4 * far - 1)

                @pl.when(far == 4)
                def _():
                    column_wait(which, 13)

            prepare(2 * far - 2)
            prepare(2 * far - 1)
            near_tile(0, NEAR, far - 1)

        @pl.when(far == 4)
        def _():
            lax.fori_loop(0, NEAR, near_out, 0)

        @pl.when(far < 4)
        def _():
            advance(far + 1)

        @pl.when(far == 1)
        def _():
            wave(2)

        @pl.when(far == 2)
        def _():
            wave(3)

        @pl.when(far == 3)
        def _():
            for block in STEPS[NEAR:EARLY]:
                for which in range(3):
                    if (which, block) not in waited:
                        take(which, block)
            lax.fori_loop(NEAR, EARLY, near_row, 0)

        if EARLY > NEAR:
            @pl.when(far >= 3)
            def _():
                near_tile(NEAR, EARLY, far - 3)

        return carry

    lax.fori_loop(1, 7 if EARLY > NEAR else 5, near_chunk, 0)
    for block in STEPS[1:]:
        for which in range(3):
            if (which, block) not in waited:
                take(which, block)
    for step in range(1, GROUP):
        group_copy(step, inputs, group_x, x_send, x_recv).start()

    lax.fori_loop(NEAR, EARLY, near_out, 0)

    def row_block(index, carry):
        step = PLANE - 1 - index
        wide = unpack_rows(row_u[step]).astype(f32)
        left = left_next[lax.rem(index, 2)]
        left_next[lax.rem(index + 1, 2)] = row_operand(jnp.maximum(step - 1, NEAR))[0]
        inner = jnp.concatenate([row_s[step], row_p[step]], axis=1)
        total = None
        block = 1024
        for start in range(0, WIDTH, block):
            p = col_p[...].reshape(WIDTH, PROBES)[start:start + block]
            part = tile(left, inner, start, block, p, mix[start:start + block, :])
            total = part if total is None else tuple(a + b for a, b in zip(total, part))
        finish_rows(step, *total, wide)
        return carry

    left_next[0] = row_operand(PLANE - 1)[0]
    lax.fori_loop(0, PLANE - EARLY, row_block, 0)

    for step in range(1, GROUP):
        group_wait(step, inputs, group_x, x_send, x_recv)
    here = pl.multiple_of(member * SLICE, SLICE)

    def group_rows(pair, carry):
        rows = group_x[pl.ds(2 * pair, 2)].reshape(2 * ROWS, IN)
        start = pl.multiple_of(pair * 2 * ROWS, 2 * ROWS)
        group_xt[:, pl.ds(start, 2 * ROWS)] = rows.T
        pre = dot(rows, w_first[:, pl.ds(here, SLICE)])
        sigma = jax.nn.sigmoid(pre)
        factor[pl.ds(start, 2 * ROWS), :] = sigma * (1.0 + pre * (1.0 - sigma))
        return carry

    lax.fori_loop(0, GROUP // 2, group_rows, 0)

    def add_up(step, totals):
        for which in range(2):
            out_copy(step, which).wait_recv()
        return totals[0] + got_v[step].astype(f32), totals[1] + got_d[step].astype(f32)

    vsum, part = lax.fori_loop(1, PLANE, add_up, (out_v[0].astype(f32), out_d[0].astype(f32)))
    products[...] = (vsum * probe_gain).astype(bf16)
    lscale = loss_gain / math.sqrt(PROBES)
    length = inv_length[...]
    dfeat = part * (-lscale * jnp.concatenate([length, length], axis=1))
    packed_d = dfeat.astype(bf16)
    group_d[member] = packed_d
    for step in range(1, GROUP):
        group_copy(step, group_d.at[member], group_d, d_send, d_recv).start()

    def place(px, py):
        return 2 * (4 * lax.rem(px, 2) + py) + lax.div(px, 2)

    def chunk_copy(step, part):
        px, py = plane_peer(step, 1)
        here = (pl.ds(0, 64 * LANES), pl.ds(64 * LANES, 32))[part]
        return remote(
            chunks.at[place(px, py), here], got_chunks.at[step, here],
            chunk_send.at[part, step], chunk_recv.at[part, step], device(px, py, z, core),
        )

    def send_chunk(part):
        def send(step, carry):
            chunk_copy(step, part).start()
            return carry

        return send

    second = dot(hidden_t[...], unpack_rows(packed_d))
    low = jnp.concatenate([second[: HID // 2], second[HID // 2:]], axis=1).astype(bf16)
    for far in range(4):
        tile = 8 * LANES + far
        chunks[:, tile * 8:tile * 8 + 8, :] = low[128 * far:128 * far + 128].reshape(PLANE, 8, 128)

    lax.fori_loop(1, PLANE, send_chunk(1), 0)
    for step in range(1, GROUP):
        group_wait(step, group_d.at[member], group_d, d_send, d_recv)
    whole_d = jnp.concatenate([unpack_rows(group_d[item]) for item in range(GROUP)], axis=0)
    back = dot(whole_d, w_second[:, pl.ds(here, SLICE)])
    dpre = (back * factor[...]).astype(bf16)
    for far in range(8):
        first = dot(group_xt[128 * far:128 * far + 128, :], dpre).astype(bf16)
        for lane in range(LANES):
            tile = far * LANES + lane
            chunks[:, tile * 8:tile * 8 + 8, :] = first[:, 128 * lane:128 * lane + 128].reshape(PLANE, 8, 128)

    lax.fori_loop(1, PLANE, send_chunk(0), 0)

    def add_chunk(step, total):
        chunk_copy(step, 1).wait_recv()
        chunk_copy(step, 0).wait_recv()
        return total + got_chunks[step].astype(f32)

    summed = lax.fori_loop(1, PLANE, add_chunk, chunks[place(x, y)].astype(f32))

    depth = 8 * LANES
    for far in range(8):
        extra = 8 * depth + 8 * (far % 4)
        pieces[far] = jnp.concatenate(
            [summed[depth * far:depth * far + depth], summed[extra:extra + 8]], axis=0
        ).astype(bf16)

    own_slot = 2 * z + core

    def piece_copy(step):
        pz, pc = column_peer(step)
        return remote(
            pieces.at[pz], got_pieces.at[own_slot], piece_send.at[step], piece_recv.at[step],
            device(x, y, pz, pc),
        )

    def send_piece(step, carry):
        piece_copy(step).start()
        return carry

    lax.fori_loop(1, COLS, send_piece, 0)
    got_pieces[own_slot] = pieces[z]

    def wait_piece(step, carry):
        pz = lax.rem(z + 8 - lax.div(step, 2), 8)
        pc = lax.rem(core + lax.rem(step, 2), 2)
        remote(pieces.at[z], got_pieces.at[2 * pz + pc], piece_send.at[step], piece_recv.at[step], me).wait_recv()
        return carry

    lax.fori_loop(1, COLS, wait_piece, 0)
    strips = []
    tail = jnp.zeros((8, 128), f32)
    for item in range(GROUP):
        total = got_pieces[item].astype(f32)
        for other in range(item + GROUP, COLS, GROUP):
            total = total + got_pieces[other].astype(f32)
        strips += [total[8 * lane:8 * lane + 8] for lane in range(LANES)]
        tail = tail + total[depth:depth + 8]
    full = jnp.concatenate(strips, axis=1)
    grad_first[...] = jnp.where(core == 0, full[:4], full[4:])
    tail = jnp.where(z < 4, tail[:, :FEAT], tail[:, FEAT:])
    grad_second[...] = jnp.where(core == 0, tail[:4], tail[4:])

    for which in range(3):
        for far in range(4):
            up_copy(which, far).wait_send()
        for far in range(3):
            down_copy(which, far).wait_send()
        for slot in (0, 1, 4, 5, 8, 9, 12, OWN):
            side_copy(which, slot, 3).wait_send()

    def finish_plane(step, carry):
        for which in range(3):
            remote(
                rows[which].at[0], rows[which].at[step],
                row_send.at[which, step], row_recv.at[which, step], me,
            ).wait_send()
        for which in range(2):
            out_copy(step, which).wait_send()
        chunk_copy(step, 0).wait_send()
        chunk_copy(step, 1).wait_send()
        return carry

    lax.fori_loop(1, PLANE, finish_plane, 0)
    for step in range(1, GROUP):
        group_copy(step, inputs, group_x, x_send, x_recv).wait_send()
        group_copy(step, group_d.at[member], group_d, d_send, d_recv).wait_send()

    def finish_column(step, carry):
        piece_copy(step).wait_send()
        return carry

    lax.fori_loop(1, COLS, finish_column, 0)


def settle(products, grad_first, grad_second, out_products, out_first, out_second):
    out_products[...] = products[...]
    out_first[...] = grad_first[...]
    out_second[...] = grad_second[...]


def local(inputs, w_first, w_second, inv_length, probes, solves):
    vmem = pl.BlockSpec(memory_space=pltpu.VMEM)
    hbm = pl.BlockSpec(memory_space=pl.ANY)
    dma = pltpu.SemaphoreType.DMA
    shapes = (
        jax.ShapeDtypeStruct((ROWS, PROBES), bf16),
        jax.ShapeDtypeStruct((4, HID), f32),
        jax.ShapeDtypeStruct((4, FEAT), f32),
    )
    results = pl.pallas_call(
        kernel,
        out_shape=shapes,
        in_specs=[hbm, hbm, hbm, vmem, hbm, hbm],
        out_specs=(vmem, vmem, vmem),
        scratch_shapes=[
            pltpu.VMEM((IN, HID), bf16),
            pltpu.VMEM((FEAT, HID), bf16),
            pltpu.VMEM((PLANE, ROWS, PROBES), bf16),
            pltpu.VMEM((PLANE, ROWS, PROBES), bf16),
            pltpu.VMEM((PLANE, HALF, 2 * FEAT), bf16),
            pltpu.VMEM((COLS, ROWS, PROBES), bf16),
            pltpu.VMEM((COLS, ROWS, PROBES), bf16),
            pltpu.VMEM((COLS, HALF, 2 * FEAT), bf16),
            pltpu.VMEM((4 * FEAT, WIDTH), bf16),
            pltpu.VMEM((2 * PROBES, WIDTH), bf16),
            pltpu.VMEM((WIDTH, FEAT), bf16),
            pltpu.VMEM((EARLY * ROWS, 4 * FEAT), bf16),
            pltpu.VMEM((2, ROWS, 4 * FEAT), bf16),
            pltpu.VMEM((EARLY * ROWS, PROBES), f32),
            pltpu.VMEM((EARLY * ROWS, FEAT), f32),
            pltpu.VMEM((EARLY * ROWS, 128), f32),
            pltpu.VMEM((PLANE, ROWS, PROBES), bf16),
            pltpu.VMEM((PLANE, HALF, 2 * FEAT), bf16),
            pltpu.VMEM((PLANE, ROWS, PROBES), bf16),
            pltpu.VMEM((PLANE, HALF, 2 * FEAT), bf16),
            pltpu.VMEM((GROUP, ROWS, IN), bf16),
            pltpu.VMEM((IN, GROWS), bf16),
            pltpu.VMEM((GROWS, SLICE), f32),
            pltpu.VMEM((HID, ROWS), bf16),
            pltpu.VMEM((GROUP, HALF, 2 * FEAT), bf16),
            pltpu.VMEM((PLANE, TILES * 8, 128), bf16),
            pltpu.VMEM((PLANE, TILES * 8, 128), bf16),
            pltpu.VMEM((8, 8 * LANES + 8, 128), bf16),
            pltpu.VMEM((COLS, 8 * LANES + 8, 128), bf16),
            dma((6,)), dma((HID // 256,)), dma((3, PLANE)), dma((3, PLANE)),
            dma((3, 4)), dma((3, 4)), dma((3, COLS)), dma((3, COLS)),
            dma((2, PLANE)), dma((2, PLANE)),
            dma((GROUP,)), dma((GROUP,)), dma((GROUP,)), dma((GROUP,)),
            dma((2, PLANE)), dma((2, PLANE)), dma((COLS,)), dma((COLS,)),
        ],
        compiler_params=pltpu.CompilerParams(
            collective_id=0, has_side_effects=True, vmem_limit_bytes=56 * 1024 * 1024
        ),
        name="gradient_step",
    )(inputs, w_first, w_second.T, inv_length.reshape(1, FEAT), probes, solves)
    return pl.pallas_call(
        settle, out_shape=shapes, in_specs=[vmem] * 3, out_specs=(vmem, vmem, vmem), name="settle"
    )(*results)


def solution(mesh):
    rows = P(("enc", "kr", "kc"), None)
    return jax.shard_map(
        local, mesh=mesh, in_specs=(rows, P(), P(), P(), rows, rows),
        out_specs=(rows, rows, rows), check_vma=False,
    )
```

```python
import functools
import math

import jax
import jax.numpy as jnp
from jax import lax
from jax.experimental import pallas as pl
from jax.experimental.pallas import tpu as pltpu
from jax.sharding import PartitionSpec as P

probe_gain = 0.5
loss_gain = 0.02

ROWS = 192
HALF = ROWS // 2
IN = 1024
HID = 1024
FEAT = 64
PROBES = 128
PLANE = 16
COLS = 16
WIDTH = COLS * ROWS
GROUP = 4
SLICE = HID // GROUP
GROWS = GROUP * ROWS
LANES = SLICE // 128
TILES = 8 * LANES + 4
LOG2E = 1.4426950408889634
MESH = pl.DeviceIdType.MESH
f32 = jnp.float32
bf16 = jnp.bfloat16


def dot(left, right):
    return jnp.dot(left, right, preferred_element_type=f32)


NEAR = 5
EARLY = 5
STEPS = (
    (0, 0), (0, 1), (0, 3), (1, 0), (3, 0), (1, 1), (3, 3), (1, 3),
    (3, 1), (0, 2), (2, 0), (2, 1), (2, 3), (1, 2), (3, 2), (2, 2),
)
PAIR = 2 * ROWS
CHUNK = 4 * ROWS
OWN = 2


def dot_nt(left, right):
    return lax.dot_general(left, right, (((1,), (1,)), ((), ())), preferred_element_type=f32)


def split3(value):
    one = value.astype(bf16)
    rest = value - one.astype(f32)
    two = rest.astype(bf16)
    three = (rest - two.astype(f32)).astype(bf16)
    return one, two, three


def unpack_rows(packed):
    return jnp.concatenate([packed[:, :FEAT], packed[:, FEAT:]], axis=0)


def pack_rows(value):
    half = value.shape[0] // 2
    return jnp.concatenate([value[:half], value[half:]], axis=1)


def half_norms(wide):
    return (-0.5 * LOG2E) * jnp.sum(wide * wide, axis=1, keepdims=True)


def extras(norms, own, other):
    one, two, three = split3(norms)
    lane = lax.broadcasted_iota(jnp.int32, (norms.shape[0], FEAT), 1)
    filled = jnp.where((lane >= other) & (lane < other + 3), 1.0, 0.0)
    filled = jnp.where(lane == own, one.astype(f32), filled)
    filled = jnp.where(lane == own + 1, two.astype(f32), filled)
    filled = jnp.where(lane == own + 2, three.astype(f32), filled)
    return filled.astype(bf16)


def kernel(
    inputs_hbm, w_first_hbm, w_second_hbm, inv_length, probes_hbm, solves_hbm,
    products, grad_first, grad_second,
    w_first, w_second, row_p, row_s, row_u, col_p, col_s, col_u, cross_t, inner_t, mix,
    left_near, left_next, near_v, near_m, near_s, out_v, out_d, got_v, got_d,
    group_x, group_xt, factor, hidden_t, group_d,
    chunks, got_chunks, pieces, got_pieces,
    load_sem, weight_sem, row_send, row_recv, up_send, down_send, side_send, col_recv,
    out_send, out_recv, x_send, x_recv, d_send, d_recv,
    chunk_send, chunk_recv, piece_send, piece_recv,
):
    z = lax.axis_index("enc")
    kr = lax.axis_index("kr")
    kc = lax.axis_index("kc")
    y = lax.rem(kr, 4)
    x = 2 * lax.div(kc, 2) + lax.div(kr, 4)
    core = lax.rem(kc, 2)

    def device(x, y, z, core):
        return (z, 4 * lax.rem(x, 2) + y, 2 * lax.div(x, 2) + core)

    def moved(dx, dy, sign):
        return lax.rem(x + 4 + sign * dx, 4), lax.rem(y + 4 + sign * dy, 4)

    def plane_peer(step, sign):
        return moved(lax.div(step, 4), lax.rem(step, 4), sign)

    def column_peer(step):
        return lax.rem(z + lax.div(step, 2), 8), lax.rem(core + lax.rem(step, 2), 2)

    def remote(src, dst, send, recv, target):
        return pltpu.make_async_remote_copy(
            src_ref=src, dst_ref=dst, send_sem=send, recv_sem=recv,
            device_id=target, device_id_type=MESH,
        )

    me = (z, kr, kc)
    sibling = device(x, y, z, 1 - core)
    up = device(x, y, lax.rem(z + 1, 8), core)
    down = device(x, y, lax.rem(z + 7, 8), core)
    z_low = lax.rem(z, 2)
    member = 2 * z_low + core

    barrier = pltpu.get_barrier_semaphore()

    loads = [
        pltpu.make_async_copy(source, target, load_sem.at[index])
        for index, (source, target) in enumerate((
            (inputs_hbm, group_x.at[member]), (w_second_hbm, w_second),
            (probes_hbm, col_p.at[OWN]), (solves_hbm, col_s.at[OWN]),
            (probes_hbm, row_p.at[0]), (solves_hbm, row_s.at[0]),
        ))
    ]

    def load_weights(block):
        here = pl.ds(pl.multiple_of(block * 256, 256), 256)
        return pltpu.make_async_copy(w_first_hbm.at[:, here], w_first.at[:, here], weight_sem.at[block])

    loads[0].start()
    for block in range(HID // 256):
        load_weights(block).start()
    for load in loads[1:]:
        load.start()

    def greet_plane(step, carry):
        px, py = plane_peer(step, 1)
        pl.semaphore_signal(barrier, inc=1, device_id=device(px, py, z, core), device_id_type=MESH)
        return carry

    def greet_column(step, carry):
        pz, pc = column_peer(step)
        pl.semaphore_signal(barrier, inc=1, device_id=device(x, y, pz, pc), device_id_type=MESH)
        return carry

    lax.fori_loop(1, PLANE, greet_plane, 0)
    lax.fori_loop(1, COLS, greet_column, 0)

    loads[0].wait()
    loads[1].wait()

    def encode(block, total):
        start = pl.multiple_of(block * 256, 256)
        load_weights(block).wait()
        pre = dot(group_x[member], w_first[:, pl.ds(start, 256)])
        hidden = (pre * jax.nn.sigmoid(pre)).astype(bf16)
        hidden_t[pl.ds(start, 256), :] = hidden.T
        return total + dot_nt(hidden, w_second[:, pl.ds(start, 256)])

    features = lax.fori_loop(0, HID // 256, encode, jnp.zeros((ROWS, FEAT), f32))
    scaled = (features * inv_length[...]).astype(bf16)
    packed = pack_rows(scaled)
    col_u[OWN] = packed
    row_u[0] = packed

    for load in loads[2:]:
        load.wait()

    pl.semaphore_wait(barrier, 30)

    columns = (col_u, col_p, col_s)
    rows = (row_u, row_p, row_s)

    def up_slot(far):
        if isinstance(far, int):
            return (OWN, 0, 4, 8, 12)[far]
        return 4 * far - 4

    def down_slot(far):
        if isinstance(far, int):
            return (OWN, 1, 5, 9)[far]
        return 4 * far - 3

    def up_copy(which, far):
        buffer = columns[which]
        return remote(
            buffer.at[up_slot(far)], buffer.at[up_slot(far + 1)],
            up_send.at[which, far], col_recv.at[which, up_slot(far + 1)], up,
        )

    def down_copy(which, far):
        buffer = columns[which]
        return remote(
            buffer.at[down_slot(far)], buffer.at[down_slot(far + 1)],
            down_send.at[which, far], col_recv.at[which, down_slot(far + 1)], down,
        )

    def side_copy(which, slot, there):
        buffer = columns[which]
        return remote(
            buffer.at[slot], buffer.at[there], side_send.at[which, slot], col_recv.at[which, there], sibling,
        )

    def column_wait(which, slot):
        buffer = columns[which]
        remote(buffer.at[slot], buffer.at[slot], side_send.at[which, 0], col_recv.at[which, slot], me).wait_recv()

    def row_send_on(which, source, dx, dy, here):
        slot = STEPS.index(here)
        px, py = moved(dx, dy, 1)
        return remote(
            rows[which].at[STEPS.index(source)], rows[which].at[slot],
            row_send.at[which, slot], row_recv.at[which, slot], device(px, py, z, core),
        )

    def row_wait(which, step):
        remote(
            rows[which].at[0], rows[which].at[step],
            row_send.at[which, step], row_recv.at[which, step], me,
        ).wait_recv()

    ways = ((1, 3), (1, 1), (0, 3))

    def offset(axis, along, across):
        return (along, across) if axis == 0 else (across, along)

    def spread(which, block):
        first, turn = ways[which]
        second = 1 - first
        along, across = block[first], block[second]
        moves = []
        if across == 0:
            if along == 0:
                moves += [(first, 1), (first, 3)]
            elif along == (4 - turn) % 4:
                moves.append((first, turn))
            moves += [(second, 1), (second, 3)]
        elif across == (4 - turn) % 4:
            moves.append((second, turn))
        for axis, way in moves:
            here = [block[0], block[1]]
            here[axis] = (here[axis] - way) % 4
            row_send_on(which, block, *offset(axis, way, 0), tuple(here)).start()

    waited = set()

    def take(which, block):
        waited.add((which, block))
        row_wait(which, STEPS.index(block))
        spread(which, block)

    def wave(level, items=(0, 1, 2)):
        for which in items:
            for block in STEPS[1:]:
                first, turn = ways[which]
                far = [0 if item == 0 else 2 if item == 2 else 1 for item in block]
                goes_on = block[1 - first] == 0 or block[1 - first] == (4 - turn) % 4
                if sum(far) == level and goes_on:
                    take(which, block)

    for which in range(3):
        up_copy(which, 0).start()
        down_copy(which, 0).start()
        spread(which, (0, 0))
        side_copy(which, OWN, OWN + 1).start()

    def advance(far, items=(0, 1, 2)):
        for which in items:
            here = up_slot(far)
            column_wait(which, here)

            @pl.when(far < 4)
            def _():
                up_copy(which, far).start()

            side_copy(which, here, jnp.where(far == 4, 13, 4 * far + 2)).start()

            @pl.when(far < 4)
            def _():
                column_wait(which, down_slot(far))

                @pl.when(far < 3)
                def _():
                    down_copy(which, far).start()

                side_copy(which, down_slot(far), 4 * far + 3).start()

    def group_copy(step, source, buffer, send, recv):
        other = lax.rem(member + step, GROUP)
        pz = z - z_low + lax.div(other, 2)
        return remote(source, buffer.at[member], send.at[step], recv.at[step], device(x, y, pz, lax.rem(other, 2)))

    def group_wait(step, source, buffer, send, recv):
        other = lax.rem(member + GROUP - step, GROUP)
        remote(source, buffer.at[other], send.at[step], recv.at[step], me).wait_recv()

    inputs = group_x.at[member]

    def row_operand(step):
        wide = unpack_rows(row_u[step]).astype(f32)
        u = wide.astype(bf16)
        return jnp.concatenate([u, u, u, extras(half_norms(wide), 0, 3)], axis=1), wide

    near_v[...] = jnp.zeros_like(near_v)
    near_m[...] = jnp.zeros_like(near_m)
    near_s[...] = jnp.zeros_like(near_s)
    def near_row(step, carry):
        left_near[pl.ds(pl.multiple_of(step * ROWS, ROWS), ROWS), :] = row_operand(step)[0]
        return carry

    for items in ((0,), (1, 2)):
        advance(1, items)
        wave(1, items)
        for block in STEPS[1:NEAR]:
            for which in items:
                if (which, block) not in waited:
                    take(which, block)
        if 0 in items:
            lax.fori_loop(0, NEAR, near_row, 0)

    def prepare(pair):
        slot = 2 * pair
        start = pl.multiple_of(slot * ROWS, PAIR)
        u = jnp.concatenate([unpack_rows(col_u[slot]), unpack_rows(col_u[slot + 1])], axis=0)
        wide = u.astype(f32)
        one, two, three = split3(wide * LOG2E)
        tail = extras(half_norms(wide), 3, 0)
        operand = jnp.concatenate([one, two, three, tail], axis=1)
        cross_t[:, pl.ds(start, PAIR)] = operand.T
        p = jnp.concatenate([col_p[slot], col_p[slot + 1]], axis=0)
        s = jnp.concatenate([col_s[slot], col_s[slot + 1]], axis=0)
        inner_t[pl.ds(0, PROBES), pl.ds(start, PAIR)] = p.T
        inner_t[pl.ds(PROBES, PROBES), pl.ds(start, PAIR)] = s.T
        mix[pl.ds(start, PAIR), :] = u

    def tile(left, inner, start, size, p, u):
        value = jnp.exp2(dot(left, cross_t[:, pl.ds(start, size)]))
        both = value * dot(inner, inner_t[:, pl.ds(start, size)])
        sums = both[:, :128]
        for lane in range(128, size, 128):
            sums = sums + both[:, lane:lane + 128]
        return dot(value.astype(bf16), p), dot(both.astype(bf16), u), sums

    def near_tile(low, high, chunk):
        size = (high - low) * ROWS
        here = pl.ds(low * ROWS, size)
        start = pl.multiple_of(chunk * CHUNK, CHUNK)
        inner = jnp.concatenate(
            [row_s[low:high].reshape(size, PROBES), row_p[low:high].reshape(size, PROBES)], axis=1
        )
        p = col_p[pl.ds(4 * chunk, 4)].reshape(CHUNK, PROBES)
        vsum, mixed, sums = tile(left_near[here, :], inner, start, CHUNK, p, mix[pl.ds(start, CHUNK), :])
        near_v[here, :] += vsum
        near_m[here, :] += mixed
        near_s[here, :] += sums

    def table(step, values):
        if isinstance(step, int):
            return values[step]
        total = 0
        for index, value in enumerate(values):
            if value:
                total = total + jnp.where(step == index, value, 0)
        return total

    def out_copy(step, which):
        dx = table(step, [item[0] for item in STEPS])
        dy = table(step, [item[1] for item in STEPS])
        px, py = moved(dx, dy, 1)
        source = (out_v, out_d)[which]
        target = (got_v, got_d)[which]
        return remote(
            source.at[step], target.at[step], out_send.at[which, step], out_recv.at[which, step],
            device(px, py, z, core),
        )

    def finish_rows(step, vsum, mixed, sums, wide):
        part = jnp.sum(sums, axis=1, keepdims=True) * wide - mixed
        out_v[step] = vsum.astype(bf16)
        out_d[step] = pack_rows(part).astype(bf16)

        @pl.when(step > 0)
        def _():
            out_copy(step, 0).start()
            out_copy(step, 1).start()

    def near_out(step, carry):
        here = pl.ds(pl.multiple_of(step * ROWS, ROWS), ROWS)
        wide = unpack_rows(row_u[step]).astype(f32)
        finish_rows(step, near_v[here, :], near_m[here, :], near_s[here, :], wide)
        return carry

    def near_chunk(far, carry):
        @pl.when(far <= 4)
        def _():
            for which in range(3):
                @pl.when(far == 1)
                def _():
                    column_wait(which, OWN + 1)

                @pl.when(far == 4)
                def _():
                    column_wait(which, 13)

            prepare(2 * far - 2)

            @pl.when(far == 1)
            def _():
                prepare(1)

            near_tile(0, NEAR, far - 1)

        @pl.when(far == 4)
        def _():
            lax.fori_loop(0, NEAR, near_out, 0)

        @pl.when(far < 4)
        def _():
            for which in range(3):
                column_wait(which, 4 * far + 2)
                column_wait(which, 4 * far + 3)
            prepare(2 * far + 1)
            advance(far + 1)

        @pl.when(far == 1)
        def _():
            wave(2)

        @pl.when(far == 2)
        def _():
            wave(3)

        @pl.when(far == 3)
        def _():
            for block in STEPS[NEAR:EARLY]:
                for which in range(3):
                    if (which, block) not in waited:
                        take(which, block)
            lax.fori_loop(NEAR, EARLY, near_row, 0)

        if EARLY > NEAR:
            @pl.when(far >= 3)
            def _():
                near_tile(NEAR, EARLY, far - 3)

        return carry

    lax.fori_loop(1, 7 if EARLY > NEAR else 5, near_chunk, 0)
    for block in STEPS[1:]:
        for which in range(3):
            if (which, block) not in waited:
                take(which, block)
    for step in range(1, GROUP):
        group_copy(step, inputs, group_x, x_send, x_recv).start()

    lax.fori_loop(NEAR, EARLY, near_out, 0)

    def row_block(index, carry):
        step = PLANE - 1 - index
        wide = unpack_rows(row_u[step]).astype(f32)
        left = left_next[lax.rem(index, 2)]
        left_next[lax.rem(index + 1, 2)] = row_operand(jnp.maximum(step - 1, NEAR))[0]
        inner = jnp.concatenate([row_s[step], row_p[step]], axis=1)
        total = None
        block = 1024
        for start in range(0, WIDTH, block):
            p = col_p[...].reshape(WIDTH, PROBES)[start:start + block]
            part = tile(left, inner, start, block, p, mix[start:start + block, :])
            total = part if total is None else tuple(a + b for a, b in zip(total, part))
        finish_rows(step, *total, wide)
        return carry

    left_next[0] = row_operand(PLANE - 1)[0]
    lax.fori_loop(0, PLANE - EARLY, row_block, 0)

    for step in range(1, GROUP):
        group_wait(step, inputs, group_x, x_send, x_recv)
    here = pl.multiple_of(member * SLICE, SLICE)

    def group_rows(pair, carry):
        rows = group_x[pl.ds(2 * pair, 2)].reshape(2 * ROWS, IN)
        start = pl.multiple_of(pair * 2 * ROWS, 2 * ROWS)
        group_xt[:, pl.ds(start, 2 * ROWS)] = rows.T
        pre = dot(rows, w_first[:, pl.ds(here, SLICE)])
        sigma = jax.nn.sigmoid(pre)
        factor[pl.ds(start, 2 * ROWS), :] = sigma * (1.0 + pre * (1.0 - sigma))
        return carry

    lax.fori_loop(0, GROUP // 2, group_rows, 0)

    def add_up(step, totals):
        for which in range(2):
            out_copy(step, which).wait_recv()
        return totals[0] + got_v[step].astype(f32), totals[1] + got_d[step].astype(f32)

    vsum, part = lax.fori_loop(1, PLANE, add_up, (out_v[0].astype(f32), out_d[0].astype(f32)))
    products[...] = (vsum * probe_gain).astype(bf16)
    lscale = loss_gain / math.sqrt(PROBES)
    length = inv_length[...]
    dfeat = part * (-lscale * jnp.concatenate([length, length], axis=1))
    packed_d = dfeat.astype(bf16)
    group_d[member] = packed_d
    for step in range(1, GROUP):
        group_copy(step, group_d.at[member], group_d, d_send, d_recv).start()

    def place(px, py):
        return 2 * (4 * lax.rem(px, 2) + py) + lax.div(px, 2)

    def chunk_copy(step, part):
        px, py = plane_peer(step, 1)
        here = (pl.ds(0, 64 * LANES), pl.ds(64 * LANES, 32))[part]
        return remote(
            chunks.at[place(px, py), here], got_chunks.at[step, here],
            chunk_send.at[part, step], chunk_recv.at[part, step], device(px, py, z, core),
        )

    def send_chunk(part):
        def send(step, carry):
            chunk_copy(step, part).start()
            return carry

        return send

    second = dot(hidden_t[...], unpack_rows(packed_d))
    low = jnp.concatenate([second[: HID // 2], second[HID // 2:]], axis=1).astype(bf16)
    for far in range(4):
        tile = 8 * LANES + far
        chunks[:, tile * 8:tile * 8 + 8, :] = low[128 * far:128 * far + 128].reshape(PLANE, 8, 128)

    lax.fori_loop(1, PLANE, send_chunk(1), 0)
    for step in range(1, GROUP):
        group_wait(step, group_d.at[member], group_d, d_send, d_recv)
    whole_d = jnp.concatenate([unpack_rows(group_d[item]) for item in range(GROUP)], axis=0)
    back = dot(whole_d, w_second[:, pl.ds(here, SLICE)])
    dpre = (back * factor[...]).astype(bf16)
    for far in range(8):
        first = dot(group_xt[128 * far:128 * far + 128, :], dpre).astype(bf16)
        for lane in range(LANES):
            tile = far * LANES + lane
            chunks[:, tile * 8:tile * 8 + 8, :] = first[:, 128 * lane:128 * lane + 128].reshape(PLANE, 8, 128)

    lax.fori_loop(1, PLANE, send_chunk(0), 0)

    def add_chunk(step, total):
        chunk_copy(step, 1).wait_recv()
        chunk_copy(step, 0).wait_recv()
        return total + got_chunks[step].astype(f32)

    summed = lax.fori_loop(1, PLANE, add_chunk, chunks[place(x, y)].astype(f32))

    depth = 8 * LANES
    for far in range(8):
        extra = 8 * depth + 8 * (far % 4)
        pieces[far] = jnp.concatenate(
            [summed[depth * far:depth * far + depth], summed[extra:extra + 8]], axis=0
        ).astype(bf16)

    own_slot = 2 * z + core

    def piece_copy(step):
        pz, pc = column_peer(step)
        return remote(
            pieces.at[pz], got_pieces.at[own_slot], piece_send.at[step], piece_recv.at[step],
            device(x, y, pz, pc),
        )

    def send_piece(step, carry):
        piece_copy(step).start()
        return carry

    lax.fori_loop(1, COLS, send_piece, 0)
    got_pieces[own_slot] = pieces[z]

    def wait_piece(step, carry):
        pz = lax.rem(z + 8 - lax.div(step, 2), 8)
        pc = lax.rem(core + lax.rem(step, 2), 2)
        remote(pieces.at[z], got_pieces.at[2 * pz + pc], piece_send.at[step], piece_recv.at[step], me).wait_recv()
        return carry

    lax.fori_loop(1, COLS, wait_piece, 0)
    strips = []
    tail = jnp.zeros((8, 128), f32)
    for item in range(GROUP):
        total = got_pieces[item].astype(f32)
        for other in range(item + GROUP, COLS, GROUP):
            total = total + got_pieces[other].astype(f32)
        strips += [total[8 * lane:8 * lane + 8] for lane in range(LANES)]
        tail = tail + total[depth:depth + 8]
    full = jnp.concatenate(strips, axis=1)
    grad_first[...] = jnp.where(core == 0, full[:4], full[4:])
    tail = jnp.where(z < 4, tail[:, :FEAT], tail[:, FEAT:])
    grad_second[...] = jnp.where(core == 0, tail[:4], tail[4:])

    for which in range(3):
        for far in range(4):
            up_copy(which, far).wait_send()
        for far in range(3):
            down_copy(which, far).wait_send()
        for slot in (0, 1, 4, 5, 8, 9, 12, OWN):
            side_copy(which, slot, 3).wait_send()

    def finish_plane(step, carry):
        for which in range(3):
            remote(
                rows[which].at[0], rows[which].at[step],
                row_send.at[which, step], row_recv.at[which, step], me,
            ).wait_send()
        for which in range(2):
            out_copy(step, which).wait_send()
        chunk_copy(step, 0).wait_send()
        chunk_copy(step, 1).wait_send()
        return carry

    lax.fori_loop(1, PLANE, finish_plane, 0)
    for step in range(1, GROUP):
        group_copy(step, inputs, group_x, x_send, x_recv).wait_send()
        group_copy(step, group_d.at[member], group_d, d_send, d_recv).wait_send()

    def finish_column(step, carry):
        piece_copy(step).wait_send()
        return carry

    lax.fori_loop(1, COLS, finish_column, 0)


def settle(products, grad_first, grad_second, out_products, out_first, out_second):
    out_products[...] = products[...]
    out_first[...] = grad_first[...]
    out_second[...] = grad_second[...]


def local(inputs, w_first, w_second, inv_length, probes, solves):
    vmem = pl.BlockSpec(memory_space=pltpu.VMEM)
    hbm = pl.BlockSpec(memory_space=pl.ANY)
    dma = pltpu.SemaphoreType.DMA
    shapes = (
        jax.ShapeDtypeStruct((ROWS, PROBES), bf16),
        jax.ShapeDtypeStruct((4, HID), f32),
        jax.ShapeDtypeStruct((4, FEAT), f32),
    )
    results = pl.pallas_call(
        kernel,
        out_shape=shapes,
        in_specs=[hbm, hbm, hbm, vmem, hbm, hbm],
        out_specs=(vmem, vmem, vmem),
        scratch_shapes=[
            pltpu.VMEM((IN, HID), bf16),
            pltpu.VMEM((FEAT, HID), bf16),
            pltpu.VMEM((PLANE, ROWS, PROBES), bf16),
            pltpu.VMEM((PLANE, ROWS, PROBES), bf16),
            pltpu.VMEM((PLANE, HALF, 2 * FEAT), bf16),
            pltpu.VMEM((COLS, ROWS, PROBES), bf16),
            pltpu.VMEM((COLS, ROWS, PROBES), bf16),
            pltpu.VMEM((COLS, HALF, 2 * FEAT), bf16),
            pltpu.VMEM((4 * FEAT, WIDTH), bf16),
            pltpu.VMEM((2 * PROBES, WIDTH), bf16),
            pltpu.VMEM((WIDTH, FEAT), bf16),
            pltpu.VMEM((EARLY * ROWS, 4 * FEAT), bf16),
            pltpu.VMEM((2, ROWS, 4 * FEAT), bf16),
            pltpu.VMEM((EARLY * ROWS, PROBES), f32),
            pltpu.VMEM((EARLY * ROWS, FEAT), f32),
            pltpu.VMEM((EARLY * ROWS, 128), f32),
            pltpu.VMEM((PLANE, ROWS, PROBES), bf16),
            pltpu.VMEM((PLANE, HALF, 2 * FEAT), bf16),
            pltpu.VMEM((PLANE, ROWS, PROBES), bf16),
            pltpu.VMEM((PLANE, HALF, 2 * FEAT), bf16),
            pltpu.VMEM((GROUP, ROWS, IN), bf16),
            pltpu.VMEM((IN, GROWS), bf16),
            pltpu.VMEM((GROWS, SLICE), f32),
            pltpu.VMEM((HID, ROWS), bf16),
            pltpu.VMEM((GROUP, HALF, 2 * FEAT), bf16),
            pltpu.VMEM((PLANE, TILES * 8, 128), bf16),
            pltpu.VMEM((PLANE, TILES * 8, 128), bf16),
            pltpu.VMEM((8, 8 * LANES + 8, 128), bf16),
            pltpu.VMEM((COLS, 8 * LANES + 8, 128), bf16),
            dma((6,)), dma((HID // 256,)), dma((3, PLANE)), dma((3, PLANE)),
            dma((3, 4)), dma((3, 4)), dma((3, COLS)), dma((3, COLS)),
            dma((2, PLANE)), dma((2, PLANE)),
            dma((GROUP,)), dma((GROUP,)), dma((GROUP,)), dma((GROUP,)),
            dma((2, PLANE)), dma((2, PLANE)), dma((COLS,)), dma((COLS,)),
        ],
        compiler_params=pltpu.CompilerParams(
            collective_id=0, has_side_effects=True, vmem_limit_bytes=56 * 1024 * 1024
        ),
        name="gradient_step",
    )(inputs, w_first, w_second.T, inv_length.reshape(1, FEAT), probes, solves)
    return pl.pallas_call(
        settle, out_shape=shapes, in_specs=[vmem] * 3, out_specs=(vmem, vmem, vmem), name="settle"
    )(*results)


def solution(mesh):
    rows = P(("enc", "kr", "kc"), None)
    return jax.shard_map(
        local, mesh=mesh, in_specs=(rows, P(), P(), P(), rows, rows),
        out_specs=(rows, rows, rows), check_vma=False,
    )
```
